256 devices in a mesh: ctx: 32 (over x_hi, z, core), head: 4 (over y), video: 2 (over x_lo).
Axes of the slice: x: 4 (x_hi: 2, x_lo: 2; x = x_hi * 2 + x_lo), y: 4, z: 8, core: 2. Of those that a mesh axis runs over, the one named last changes fastest.
Arguments:
- queries: bfloat16 [2, 256, 3584], P('video', 'ctx', 'head'), may hold values from -6 to 6
- keys: bfloat16 [2, 4096, 512], P('video', 'ctx', 'head'), may hold values from -6 to 6
- values: bfloat16 [2, 4096, 512], P('video', 'ctx', 'head'), may hold values from -6 to 6
- dout: bfloat16 [2, 256, 3584], P('video', 'ctx', 'head'), may hold values from -192 to 192
- lengths: int32 [2], P('video'), may hold values from 8 to 32, as said below
- owner: int32 [2, 32], P('video', 'ctx'), may hold values from 0 to 31, as said below
- enc_rows: bfloat16 [2, 8192, 3584], P('video', 'ctx'), may hold values from -1.5 to 1.5
- w_kv: bfloat16 [3584, 1024], P(None, 'head'), may hold values from -0.09375 to 0.09375
Outputs:
- dq: bfloat16 [2, 256, 3584], P('video', 'ctx', 'head')
- enc_grad: bfloat16 [2, 8192, 3584], P('video', 'ctx', 'head')
- weight_grad: float32 [3584, 1024], P(('ctx', 'video'), 'head')
The draws below stay inside these ranges and needn't reach their ends.
Inputs may be any that keep to these rules, and one draw needn't show every extreme that they name: In every draw some video has lengths equal to 32. With P = 32 and c = b, owner[v, b] is (c - 1) mod P or (c + 1) mod P; in every video some owner receives all blocks of both neighbours, 2 blocks. In some video whose length is 32, the first block of index P - 1 is owned by 0.
All inputs are finite; a program needn't handle non-finite values.
Results may differ from the reference program's by a relative error of at most 0.009.
Values may be sent and summed in bfloat16 or wider, within the bound.
A program may use at most 64 MiB of HBM per device.

```python
import math
import jax
import jax.numpy as jnp
from jax import lax

D = 3584
QH = 28
KVH = 4
HD = 128
BLOCK = 128
VIS_DEV = 128
QPG = 7
TEXT = 256
VIS = 4096
VIDEOS = 2
N_CTX = 32


def full_choice(key):
    return jax.random.randint(jax.random.fold_in(key, 22), (), 0, VIDEOS)


def draw_queries(key, part):
    array_shape = (VIDEOS, TEXT, QH * HD)
    drawn_values = jnp.clip(jax.random.normal(jax.random.fold_in(key, 1), array_shape, jnp.float32), -6.0, 6.0)
    return drawn_values.astype(jnp.bfloat16)


def draw_keys(key, part):
    array_shape = (VIDEOS, VIS, KVH * HD)
    drawn_values = jnp.clip(jax.random.normal(jax.random.fold_in(key, 3), array_shape, jnp.float32), -6.0, 6.0)
    return drawn_values.astype(jnp.bfloat16)


def draw_lengths(key, part):
    blocks = VIS // BLOCK
    drawn_lengths = jax.random.randint(jax.random.fold_in(key, 21), (VIDEOS,), blocks // 4, blocks + 1)
    full_video = full_choice(key)
    return jnp.where(jnp.arange(VIDEOS) == full_video, blocks, drawn_lengths).astype(jnp.int32)


def draw_owner(key, part):
    per_device = VIS_DEV // BLOCK
    blocks = VIS // BLOCK
    cycle_size = VIS // VIS_DEV
    full_video = full_choice(key)
    is_full = (jnp.arange(VIDEOS, dtype=jnp.int32) == full_video)[:, None]
    coin_flips = jax.random.randint(jax.random.fold_in(key, 31), (VIDEOS, blocks), 0, 2)
    target_any = jax.random.randint(jax.random.fold_in(key, 32), (VIDEOS, 1), 0, cycle_size)
    target_full = jax.random.randint(jax.random.fold_in(key, 33), (VIDEOS, 1), 0, cycle_size - 2)
    target = jnp.where(is_full, target_full, target_any)
    device = (jnp.arange(blocks, dtype=jnp.int32) // per_device)[None, :]
    coin_flips = jnp.where(device == (target - 1) % cycle_size, 1, coin_flips)
    coin_flips = jnp.where(device == (target + 1) % cycle_size, 0, coin_flips)
    last_first = (jnp.arange(blocks, dtype=jnp.int32) == (cycle_size - 1) * per_device)[None, :]
    coin_flips = jnp.where(jnp.logical_and(is_full, last_first), 1, coin_flips)
    return ((device + 2 * coin_flips - 1) % cycle_size).astype(jnp.int32)


def level_of(stream_key, dims, split, smallest, largest):
    gain, own = 1.0, jax.random.fold_in(stream_key, 6)
    for dim, shards_of in split:
        heights = jnp.exp(jax.random.uniform(jax.random.fold_in(own, dim), (shards_of,), jnp.float32, smallest / len(split), largest / len(split)))
        gain = gain * jnp.repeat(heights, dims[dim] // shards_of).reshape([-1 if axis == dim else 1 for axis in range(len(dims))])
    return gain


def centred(key, dims, spread, limit, shards=(), kind=jnp.bfloat16):
    result = spread * jax.random.normal(key, dims, jnp.float32)
    if shards:
        result = result * level_of(key, dims, shards, -0.22, 0.18)
    return jnp.clip(result, -limit, limit).astype(kind)


def setup_inputs(seed: int = 0) -> dict:
    streams_of = jax.random.split(jax.random.key(seed), 9)
    return {
        "queries": draw_queries(jax.random.fold_in(streams_of[8], 71), 0),
        "keys": draw_keys(jax.random.fold_in(streams_of[8], 71), 0),
        "values": centred(streams_of[2], (VIDEOS, VIS, KVH * HD), 1.0, 6.0, ((0, 2), (1, 32), (2, 4))),
        "dout": centred(streams_of[3], (VIDEOS, TEXT, QH * HD), (VIS // 128), 192.0, ((0, 2), (1, 32), (2, 4))),
        "lengths": draw_lengths(jax.random.fold_in(streams_of[8], 71), 0),
        "owner": draw_owner(jax.random.fold_in(streams_of[8], 71), 0),
        "enc_rows": centred(streams_of[6], (VIDEOS, 2 * VIS, D), 0.1, 1.5, ((0, 2), (1, 32))),
        "w_kv": centred(streams_of[7], (D, KVH * 2 * HD), D ** -0.5, 0.09375, ((1, 4),)),
    }


def head_grads(query_group, key_head, value_head, dout_group, key_valid):
    factor = 1.0 / math.sqrt(HD)
    query_rows = query_group.reshape(TEXT * QPG, HD)
    dout_rows = dout_group.reshape(TEXT * QPG, HD)
    scores = jnp.dot(query_rows, key_head.T, preferred_element_type=jnp.float32) * factor
    grad_prob = jnp.dot(dout_rows, value_head.T, preferred_element_type=jnp.float32)
    masked = jnp.where(key_valid[None, :], scores, -1e+30)
    row_max = lax.optimization_barrier(jnp.max(masked, axis=1, keepdims=True))
    exp_terms = jnp.where(key_valid[None, :], jnp.exp(masked - row_max), 0.0)
    row_total = lax.optimization_barrier(jnp.sum(exp_terms, axis=1, keepdims=True))
    row_inner = lax.optimization_barrier(jnp.sum(exp_terms * grad_prob, axis=1, keepdims=True))
    attention = exp_terms / row_total
    grad_score = attention * (grad_prob - row_inner / row_total)
    attention_low = attention.astype(jnp.bfloat16)
    score_low = grad_score.astype(jnp.bfloat16)
    query_grad = jnp.dot(score_low, key_head, preferred_element_type=jnp.float32) * factor
    key_grad = jnp.dot(score_low.T, query_rows, preferred_element_type=jnp.float32) * factor
    value_grad = jnp.dot(attention_low.T, dout_rows, preferred_element_type=jnp.float32)
    key_value = jnp.concatenate([key_grad, value_grad], axis=1).astype(jnp.bfloat16)
    return (query_grad.reshape(TEXT, QPG * HD).astype(jnp.bfloat16), key_value)

def route_rows(key_value, owner_row):
    per_device = VIS_DEV // BLOCK
    device = jnp.arange(VIS // BLOCK, dtype=jnp.int32) // per_device
    goes_next = (owner_row == (device + 1) % N_CTX).reshape(N_CTX, per_device, 1, 1)
    blocks = key_value.reshape(N_CTX, per_device, BLOCK, 2 * HD * KVH)
    zero_blocks = jnp.zeros_like(blocks)
    from_before = jnp.roll(jnp.where(goes_next, blocks, zero_blocks), 1, axis=0)
    from_after = jnp.roll(jnp.where(goes_next, zero_blocks, blocks), -1, axis=0)
    return jnp.concatenate([from_before, from_after], axis=1).reshape(2 * VIS, KVH * 2 * HD)

def project(routed, w_kv):
    slots = routed.reshape(N_CTX, 2 * VIS_DEV, KVH, 2 * HD)
    weights = w_kv.reshape(D, KVH, 2 * HD)

    def owner_rows(slot_rows):
        summed = jnp.zeros((2 * VIS_DEV, D), jnp.float32)
        for head_group in range(KVH):
            head_term = jnp.dot(slot_rows[:, head_group], weights[:, head_group].T, preferred_element_type=jnp.float32)
            summed = summed + lax.optimization_barrier(head_term.astype(jnp.bfloat16)).astype(jnp.float32)
        return summed.astype(jnp.bfloat16)
    return lax.map(owner_rows, slots).reshape(2 * VIS, D)

def reference(queries, keys, values, dout, lengths, owner, enc_rows, w_kv):
    query_list = []
    encoder_list = []
    weight_grad = jnp.zeros((D, KVH * 2 * HD), jnp.float32)
    for video_index in range(VIDEOS):
        key_valid = jnp.arange(VIS, dtype=jnp.int32) // BLOCK < lengths[video_index]
        query_heads = queries[video_index].reshape(TEXT, KVH, QPG * HD).transpose(1, 0, 2)
        dout_heads = dout[video_index].reshape(TEXT, KVH, QPG * HD).transpose(1, 0, 2)
        key_heads = keys[video_index].reshape(VIS, KVH, HD).transpose(1, 0, 2)
        value_heads = values[video_index].reshape(VIS, KVH, HD).transpose(1, 0, 2)

        def one_head(arrays):
            return head_grads(arrays[0], arrays[1], arrays[2], arrays[3], key_valid)
        query_grad, key_value = lax.map(one_head, (query_heads, key_heads, value_heads, dout_heads))
        query_list.append(query_grad.transpose(1, 0, 2).reshape(TEXT, QH * HD))
        key_value = key_value.transpose(1, 0, 2).reshape(VIS, KVH * 2 * HD)
        routed = route_rows(key_value, owner[video_index])
        encoder_list.append(project(routed, w_kv))
        weight_grad = weight_grad + jnp.dot(enc_rows[video_index].T, routed, preferred_element_type=jnp.float32)
    return (jnp.stack(query_list), jnp.stack(encoder_list), weight_grad)
```

```python
import math

import jax
import jax.numpy as jnp
from jax import lax
from jax.experimental import pallas as pl
from jax.experimental.pallas import tpu as pltpu
from jax.sharding import PartitionSpec as P

NZ = 8
NC = 32
NH = 4
HD = 128
BLK = 128
QPG = 7
PIECE = 56
F32 = jnp.float32
BF16 = jnp.bfloat16
MESH = pl.DeviceIdType.MESH


def each(start, stop, fn):
    def step(i, carry):
        fn(i)
        return carry

    lax.fori_loop(start, stop, step, 0)


def nt(a, b):
    return lax.dot_general(a, b, (((1,), (1,)), ((), ())), preferred_element_type=F32)


def tn(a, b):
    return lax.dot_general(a, b, (((0,), (0,)), ((), ())), preferred_element_type=F32)


def kernel(
    q_ref, k_ref, v_ref, do_ref, len_ref, own_ref, enc_ref, w_ref,
    dq_ref, eg_ref, wg_ref,
    qv, dov, qg, kb, vb, encv, enct, encb, wb, st, cs, es, dp,
    dkvp, dkvr, dkvf, dkvg, hg, dqp, dqr, egs, wgs, wgr,
    lsem, q_s, q_r, kv_s, kv_r, st_s, st_r, dq_s, dq_r, rs_s, rs_r,
    gx_s, gx_r, gc_s, gc_r, e_s, e_r, w_s, w_r, h_s, h_r, o_s, o_r, wg_s, wg_r,
):
    factor = 1.0 / math.sqrt(HD)
    c = lax.axis_index("ctx")
    h = lax.axis_index("head")
    v = lax.axis_index("video")
    xh, z, k = lax.div(c, 2 * NZ), lax.rem(lax.div(c, 2), NZ), lax.rem(c, 2)
    xo, ko = 1 - xh, 1 - k
    c_next, c_prev = lax.rem(c + 1, NC), lax.rem(c + NC - 1, NC)
    c_cross = lax.rem(c + 2 * k - 1 + NC, NC)
    zt, xt = lax.rem(lax.div(c_cross, 2), NZ), lax.div(c_cross, 2 * NZ)

    def cid(a, b, d):
        return (a * NZ + b) * 2 + d

    def at(ctx, head, video):
        return {"ctx": ctx, "head": head, "video": video}

    def remote(src, dst, ssem, rsem, dev):
        return pltpu.make_async_remote_copy(
            src_ref=src, dst_ref=dst, send_sem=ssem, recv_sem=rsem,
            device_id=dev, device_id_type=MESH,
        )

    here = at(c, h, v)

    def zpeer(j):
        return lax.rem(z + j, NZ)

    def ppeer(d):
        return (
            lax.rem(xh + lax.div(d, 4), 2),
            lax.rem(k + lax.rem(lax.div(d, 2), 2), 2),
            lax.rem(v + lax.rem(d, 2), 2),
        )

    def bid(a, b, d):
        return a * 4 + b * 2 + d

    barrier = pltpu.get_barrier_semaphore()

    def signal(dev):
        pl.semaphore_signal(barrier, inc=1, device_id=dev, device_id_type=MESH)

    each(1, NZ, lambda j: signal(at(cid(xh, zpeer(j), k), h, v)))

    def sig_plane(d):
        a, b, e = ppeer(d)
        signal(at(cid(a, z, b), h, e))

    each(1, 8, sig_plane)

    def sig_cross(d):
        a, b, e = ppeer(d)
        signal(at(lax.rem(cid(a, z, b) + 2 * b - 1 + NC, NC), h, e))

    each(0, 8, sig_cross)
    each(1, NH, lambda j: signal(at(c, lax.rem(h + j, NH), v)))

    own4 = xh * 2 + k
    wrows = pl.ds(pl.multiple_of(h * 896, 128), 896)
    loads = [
        pltpu.make_async_copy(q_ref, qv, lsem.at[0]),
        pltpu.make_async_copy(do_ref, dov, lsem.at[1]),
        pltpu.make_async_copy(k_ref, kb.at[own4], lsem.at[2]),
        pltpu.make_async_copy(v_ref, vb.at[own4], lsem.at[3]),
        pltpu.make_async_copy(enc_ref, encv, lsem.at[4]),
        pltpu.make_async_copy(w_ref.at[wrows], wb.at[h], lsem.at[5]),
    ]
    for load in loads:
        load.start()
    loads[0].wait()
    loads[1].wait()
    pad = jnp.zeros((8, HD), F32)
    for side, ref in ((0, qv), (1, dov)):
        rows = ref[...].astype(F32)
        parts = [rows[:, g * HD : (g + 1) * HD] for g in range(QPG)] + [pad]
        qg[z, side] = jnp.concatenate(parts, axis=0).astype(BF16)

    pl.semaphore_wait(barrier, 25)

    def q_copy(j):
        zd = zpeer(j)
        return remote(qg.at[z], qg.at[z], q_s.at[zd], q_r.at[z], at(cid(xh, zd, k), h, v))

    each(1, NZ, lambda j: q_copy(j).start())

    def kv_peer(d):
        return lax.rem(xh + lax.div(d, 2), 2), lax.rem(k + lax.rem(d, 2), 2)

    def kv_copy(d, side):
        a, b = kv_peer(d)
        src, dst = ((k_ref, kb), (v_ref, vb))[side]
        return remote(
            src, dst.at[own4], kv_s.at[side, a * 2 + b], kv_r.at[side, own4], at(cid(a, z, b), h, v)
        )

    for side in (0, 1):
        each(1, 4, lambda d: kv_copy(d, side).start())

    def w_copy(j):
        hd = lax.rem(h + j, NH)
        rows = pl.ds(pl.multiple_of(hd * 896, 128), 896)
        return remote(w_ref.at[rows], wb.at[h], w_s.at[hd], w_r.at[h], at(c, hd, v))

    each(1, NH, lambda j: w_copy(j).start())

    row = lax.broadcasted_iota(jnp.int32, (1024, 896), 0)
    col = lax.broadcasted_iota(jnp.int32, (1024, 896), 1)
    inner_row = lax.rem(row, 256)
    quarter = lax.div(row, 256)
    step_of = (
        (inner_row >= PIECE).astype(jnp.int32)
        + (inner_row >= 2 * PIECE).astype(jnp.int32)
        + (inner_row >= 3 * PIECE).astype(jnp.int32)
    )
    source = step_of * (4 * PIECE) + quarter * PIECE + inner_row - step_of * PIECE
    pick = jnp.where((col == source) & (inner_row < 4 * PIECE), 1.0, 0.0).astype(BF16)
    loads[4].wait()
    for g in range(4):
        turned = nt(pick, encv[:, g * 896 : (g + 1) * 896]).astype(BF16)
        for slot in (0, 1):
            for t in range(4):
                enct[slot, g // 2, t, (g % 2) * 256 : (g % 2) * 256 + 256] = turned[
                    t * 256 : (t + 1) * 256, slot * 128 : (slot + 1) * 128
                ]

    def lanes(side):
        return pl.ds(side * 128, 128)

    b_same, b_cross = bid(xh, ko, v), bid(xt, ko, v)

    def enc_same(d):
        a, b, e = ppeer(d)
        return remote(
            enct.at[ko, a, b * 2 + e], encb.at[b_same, :, lanes(0)],
            e_s.at[0, d], e_r.at[0, b_same], at(cid(a, z, b), h, e),
        )

    def enc_cross(d):
        a, b, e = ppeer(d)
        return remote(
            enct.at[k, a, b * 2 + e], encb.at[b_cross, :, lanes(1)],
            e_s.at[1, d], e_r.at[1, b_cross], at(cid(a, zt, b), h, e),
        )

    enc_own = pltpu.make_async_copy(
        enct.at[ko, xh, k * 2 + v], encb.at[b_same, :, lanes(0)], lsem.at[6]
    )
    each(1, 8, lambda d: enc_same(d).start())
    enc_own.start()

    def q_arrived(j):
        zs = zpeer(j)
        remote(qg.at[zs], qg.at[zs], q_s.at[zs], q_r.at[zs], here).wait_recv()

    def kv_arrived(d):
        a, b = kv_peer(d)
        i = a * 2 + b
        remote(k_ref, kb.at[i], kv_s.at[0, i], kv_r.at[0, i], here).wait_recv()
        remote(v_ref, vb.at[i], kv_s.at[1, i], kv_r.at[1, i], here).wait_recv()

    loads[2].wait()
    loads[3].wait()
    each(1, 4, kv_arrived)
    each(1, NZ, q_arrived)
    keys = kb[...].reshape(512, HD)
    queries = qg[:, 0].reshape(512, HD)
    dout = qg[:, 1].reshape(512, HD)
    block = lax.div(lax.broadcasted_iota(jnp.int32, (512, 512), 0), BLK)
    place = lax.div(block, 2) * (2 * NZ) + z * 2 + lax.rem(block, 2)
    valid = place < len_ref[0]
    masked = jnp.where(valid, nt(keys, queries) * factor, -1e30)
    top = jnp.max(masked, axis=0, keepdims=True)
    terms = jnp.where(valid, jnp.exp(masked - top), 0.0)
    grad_prob = nt(vb[...].reshape(512, HD), dout)
    es[...] = terms
    dp[...] = grad_prob
    total = jnp.sum(terms, axis=0, keepdims=True)
    inner = jnp.sum(terms * grad_prob, axis=0, keepdims=True)
    for n, value in enumerate((top, total, inner)):
        for t in range(4):
            st[z, n * 4 + t : n * 4 + t + 1, :] = value[:, t * 128 : (t + 1) * 128]

    def st_copy(j):
        zd = zpeer(j)
        return remote(st.at[z], st.at[z], st_s.at[zd], st_r.at[z], at(cid(xh, zd, k), h, v))

    def st_arrived(j):
        zs = zpeer(j)
        remote(st.at[zs], st.at[zs], st_s.at[zs], st_r.at[zs], here).wait_recv()

    each(1, NZ, lambda j: st_copy(j).start())
    each(0, 8, lambda d: enc_cross(d).start())
    each(1, NZ, st_arrived)
    tops, totals, inners = st[:, 0:4, :], st[:, 4:8, :], st[:, 8:12, :]
    upper = jnp.max(tops, axis=0)
    scales = jnp.exp(tops - upper[None])
    sum_total = jnp.sum(totals * scales, axis=0)
    sum_inner = jnp.sum(inners * scales, axis=0)
    cs[0:4, :] = jnp.exp(st[z, 0:4, :] - upper) / sum_total
    cs[4:8, :] = sum_inner / sum_total
    scale = jnp.concatenate([cs[t : t + 1, :] for t in range(4)], axis=1)
    ratio = jnp.concatenate([cs[t : t + 1, :] for t in range(4, 8)], axis=1)
    attention = es[...] * scale
    score_low = (attention * (dp[...] - ratio)).astype(BF16)
    attention_low = attention.astype(BF16)
    key_grad = jnp.dot(score_low, queries, preferred_element_type=F32) * factor
    value_grad = jnp.dot(attention_low, dout, preferred_element_type=F32)
    key_value = jnp.concatenate([key_grad, value_grad], axis=1).reshape(4, BLK, 256)
    dkvf[...] = key_value
    dkvp[...] = key_value.astype(BF16)

    def rs_copy(d):
        a, b = kv_peer(d)
        i = a * 2 + b
        return remote(dkvp.at[i], dkvr.at[own4], rs_s.at[i], rs_r.at[own4], at(cid(a, z, b), h, v))

    def rs_arrived(d):
        a, b = kv_peer(d)
        i = a * 2 + b
        remote(dkvp.at[i], dkvr.at[i], rs_s.at[i], rs_r.at[i], here).wait_recv()

    each(1, 4, lambda d: rs_copy(d).start())

    dqp[...] = tn(score_low, keys).reshape(NZ, 64, HD).astype(BF16)

    def dq_copy(j):
        zd = zpeer(j)
        return remote(dqp.at[zd], dqr.at[z], dq_s.at[zd], dq_r.at[z], at(cid(xh, zd, k), h, v))

    def dq_arrived(j):
        zs = zpeer(j)
        remote(dqp.at[zs], dqr.at[zs], dq_s.at[zs], dq_r.at[zs], here).wait_recv()

    each(1, NZ, lambda j: dq_copy(j).start())
    each(1, 4, rs_arrived)
    mine = dkvf[own4]
    for d in range(1, 4):
        a, b = kv_peer(d)
        mine = mine + dkvr[a * 2 + b].astype(F32)
    mine = mine.astype(BF16)
    owner = own_ref[0, 0]
    b_me = bid(xh, k, v)
    to_same = jnp.where(jnp.full((16, 256), owner, jnp.int32) == c + 1 - 2 * k, 1.0, 0.0)
    dkvg[b_me, 0:128, :] = mine
    dkvg[b_me, 128:144, :] = to_same.astype(BF16)
    hg[h] = mine

    def gx_peer(d):
        return lax.rem(xh + lax.div(d, 2), 2), lax.rem(v + lax.rem(d, 2), 2)

    def gx_copy(d):
        a, e = gx_peer(d)
        return remote(
            dkvg.at[b_me], dkvg.at[b_me], gx_s.at[a * 2 + e], gx_r.at[xh * 2 + v],
            at(cid(a, z, k), h, e),
        )

    def gc_copy(d):
        a, e = gx_peer(d)
        i = bid(a, k, e)
        return remote(
            dkvg.at[i], dkvg.at[i], gc_s.at[a * 2 + e], gc_r.at[a * 2 + e], at(cid(xh, z, ko), h, v)
        )

    def h_copy(j):
        hd = lax.rem(h + j, NH)
        return remote(hg.at[h], hg.at[h], h_s.at[hd], h_r.at[h], at(c, hd, v))

    each(1, 4, lambda d: gx_copy(d).start())
    each(1, NH, lambda j: h_copy(j).start())
    gc_copy(0).start()

    def forward(d):
        a, e = gx_peer(d)
        i = bid(a, k, e)
        remote(
            dkvg.at[i], dkvg.at[i], gx_s.at[a * 2 + e], gx_r.at[a * 2 + e], here
        ).wait_recv()
        gc_copy(d).start()

    each(1, 4, forward)

    def h_arrived(j):
        hs = lax.rem(h + j, NH)
        remote(hg.at[hs], hg.at[hs], h_s.at[hs], h_r.at[hs], here).wait_recv()

    def w_arrived(j):
        hs = lax.rem(h + j, NH)
        remote(w_ref.at[wrows], wb.at[hs], w_s.at[hs], w_r.at[hs], here).wait_recv()

    loads[5].wait()
    each(1, NH, w_arrived)
    each(1, NH, h_arrived)
    summed = jnp.zeros((BLK, 896), F32)
    for g in range(NH):
        summed = summed + nt(hg[g], wb[g]).astype(BF16).astype(F32)
    owners = jnp.full((BLK, 896), owner, jnp.int32)
    egs[0] = jnp.where(owners == c_next, summed, 0.0).astype(BF16)
    egs[1] = jnp.where(owners == c_next, 0.0, summed).astype(BF16)
    out_next = remote(
        egs.at[0], eg_ref.at[pl.ds(0, 128)], o_s.at[0], o_r.at[0], at(c_next, h, v)
    )
    out_prev = remote(
        egs.at[1], eg_ref.at[pl.ds(128, 128)], o_s.at[1], o_r.at[1], at(c_prev, h, v)
    )
    out_next.start()
    out_prev.start()

    def gc_arrived(d):
        a, e = gx_peer(d)
        i = bid(a, ko, e)
        remote(dkvg.at[i], dkvg.at[i], gc_s.at[a * 2 + e], gc_r.at[a * 2 + e], here).wait_recv()

    def enc_arrived(side, a, b, e):
        i = bid(a, b, e)
        remote(
            enct.at[0, 0, 0], encb.at[i, :, lanes(side)], e_s.at[side, 0], e_r.at[side, i], here
        ).wait_recv()

    def same_arrived(d):
        a, b, e = ppeer(d)
        enc_arrived(0, a, 1 - b, e)

    each(0, 4, gc_arrived)
    enc_own.wait()
    each(1, 8, same_arrived)
    each(0, 8, lambda d: enc_arrived(1, *ppeer(d)))
    acc = jnp.zeros((512, 256), F32)
    for i in range(8):
        grads = dkvg[i, 0:128, :].astype(F32)
        flag = dkvg[i, 128:144, :].astype(F32)[0:1, :]
        both = jnp.concatenate([grads * flag, grads * (1.0 - flag)], axis=0).astype(BF16)
        acc = acc + jnp.dot(encb[i], both, preferred_element_type=F32)
    for t in range(NZ):
        first = (t // 4) * 256 + (t % 4) * PIECE
        wgs[t] = acc[first : first + 64].astype(BF16)

    def wg_copy(j):
        zd = zpeer(j)
        return remote(wgs.at[zd], wgr.at[z], wg_s.at[zd], wg_r.at[z], at(cid(xh, zd, k), h, v))

    def wg_arrived(j):
        zs = zpeer(j)
        remote(wgs.at[zs], wgr.at[zs], wg_s.at[zs], wg_r.at[zs], here).wait_recv()

    each(1, NZ, lambda j: wg_copy(j).start())

    each(1, NZ, dq_arrived)
    query_grad = dqp[z].astype(F32)
    for j in range(1, NZ):
        query_grad = query_grad + dqr[zpeer(j)].astype(F32)
    query_grad = query_grad * factor
    dq_ref[...] = jnp.concatenate(
        [query_grad[g * 8 : (g + 1) * 8] for g in range(QPG)], axis=1
    ).astype(BF16)

    each(1, NZ, wg_arrived)
    weight = wgs[z].astype(F32)
    for j in range(1, NZ):
        weight = weight + wgr[zpeer(j)].astype(F32)
    wg_ref[...] = weight[:PIECE]

    out_next.wait_recv()
    out_prev.wait_recv()
    each(1, NZ, lambda j: q_copy(j).wait_send())
    for side in (0, 1):
        each(1, 4, lambda d: kv_copy(d, side).wait_send())
    each(1, NH, lambda j: w_copy(j).wait_send())
    each(1, 8, lambda d: enc_same(d).wait_send())
    each(0, 8, lambda d: enc_cross(d).wait_send())
    each(1, NZ, lambda j: st_copy(j).wait_send())
    each(1, 4, lambda d: rs_copy(d).wait_send())
    each(1, NZ, lambda j: dq_copy(j).wait_send())
    each(1, 4, lambda d: gx_copy(d).wait_send())
    each(0, 4, lambda d: gc_copy(d).wait_send())
    each(1, NH, lambda j: h_copy(j).wait_send())
    out_next.wait_send()
    out_prev.wait_send()
    each(1, NZ, lambda j: wg_copy(j).wait_send())


def per_device(queries, keys, values, dout, lengths, owner, enc_rows, w_kv):
    dma = pltpu.SemaphoreType.DMA
    vmem = pltpu.VMEM
    hbm = pl.BlockSpec(memory_space=pl.ANY)
    smem = pl.BlockSpec(memory_space=pltpu.SMEM)
    out = pl.BlockSpec(memory_space=pltpu.VMEM)
    dq, eg, wg = pl.pallas_call(
        kernel,
        out_shape=(
            jax.ShapeDtypeStruct((8, 896), BF16),
            jax.ShapeDtypeStruct((256, 896), BF16),
            jax.ShapeDtypeStruct((PIECE, 256), F32),
        ),
        in_specs=[hbm, hbm, hbm, hbm, smem, smem, hbm, hbm],
        out_specs=(out, hbm, out),
        scratch_shapes=[
            vmem((8, 896), BF16),
            vmem((8, 896), BF16),
            vmem((NZ, 2, 64, HD), BF16),
            vmem((4, BLK, HD), BF16),
            vmem((4, BLK, HD), BF16),
            vmem((256, 3584), BF16),
            vmem((2, 2, 4, 512, 128), BF16),
            vmem((8, 512, 256), BF16),
            vmem((NH, 896, 256), BF16),
            vmem((NZ, 16, 128), F32),
            vmem((8, 128), F32),
            vmem((512, 512), F32),
            vmem((512, 512), F32),
            vmem((4, BLK, 256), BF16),
            vmem((4, BLK, 256), BF16),
            vmem((4, BLK, 256), F32),
            vmem((8, 144, 256), BF16),
            vmem((NH, BLK, 256), BF16),
            vmem((NZ, 64, HD), BF16),
            vmem((NZ, 64, HD), BF16),
            vmem((2, BLK, 896), BF16),
            vmem((NZ, 64, 256), BF16),
            vmem((NZ, 64, 256), BF16),
            dma((7,)),
            dma((NZ,)), dma((NZ,)),
            dma((2, 4)), dma((2, 4)),
            dma((NZ,)), dma((NZ,)),
            dma((NZ,)), dma((NZ,)),
            dma((4,)), dma((4,)),
            dma((4,)), dma((4,)),
            dma((4,)), dma((4,)),
            dma((2, 8)), dma((2, 8)),
            dma((NH,)), dma((NH,)),
            dma((NH,)), dma((NH,)),
            dma((2,)), dma((2,)),
            dma((NZ,)), dma((NZ,)),
        ],
        compiler_params=pltpu.CompilerParams(
            collective_id=0, has_side_effects=True, vmem_limit_bytes=60 * 1024 * 1024
        ),
    )(queries[0], keys[0], values[0], dout[0], lengths, owner, enc_rows[0], w_kv)
    return dq[None], eg[None], wg


def solution(mesh):
    placed = (
        P("video", "ctx", "head"),
        P("video", "ctx", "head"),
        P("video", "ctx", "head"),
        P("video", "ctx", "head"),
        P("video"),
        P("video", "ctx"),
        P("video", "ctx", None),
        P(None, "head"),
    )
    return jax.shard_map(
        per_device,
        mesh=mesh,
        in_specs=placed,
        out_specs=(
            P("video", "ctx", "head"),
            P("video", "ctx", "head"),
            P(("ctx", "video"), "head"),
        ),
        check_vma=False,
    )
```

```python
import math

import jax
import jax.numpy as jnp
from jax import lax
from jax.experimental import pallas as pl
from jax.experimental.pallas import tpu as pltpu
from jax.sharding import PartitionSpec as P

NZ = 8
NC = 32
NH = 4
HD = 128
BLK = 128
QPG = 7
PIECE = 56
F32 = jnp.float32
BF16 = jnp.bfloat16
MESH = pl.DeviceIdType.MESH


def each(start, stop, fn):
    def step(i, carry):
        fn(i)
        return carry

    lax.fori_loop(start, stop, step, 0)


def nt(a, b):
    return lax.dot_general(a, b, (((1,), (1,)), ((), ())), preferred_element_type=F32)


def tn(a, b):
    return lax.dot_general(a, b, (((0,), (0,)), ((), ())), preferred_element_type=F32)


def kernel(
    q_ref, k_ref, v_ref, do_ref, len_ref, own_ref, enc_ref, w_ref,
    dq_ref, eg_ref, wg_ref,
    qv, dov, qg, kb, vb, cand, encs, encb, wb, st, cs, es, dp,
    dkvp, dkvr, dkvf, dkvg, hg, dqp, dqr, egs, wgs, wgr,
    lsem, q_s, q_r, kv_s, kv_r, st_s, st_r, dq_s, dq_r, rs_s, rs_r,
    gx_s, gx_r, gc_s, gc_r, c_s, c_r, ex_s, ex_r, ey_s, ey_r,
    w_s, w_r, wf_s, wf_r, h_s, h_r, o_s, o_r, wg_s, wg_r,
):
    factor = 1.0 / math.sqrt(HD)
    c = lax.axis_index("ctx")
    h = lax.axis_index("head")
    v = lax.axis_index("video")
    xh, z, k = lax.div(c, 2 * NZ), lax.rem(lax.div(c, 2), NZ), lax.rem(c, 2)
    ko = 1 - k
    c_next, c_prev = lax.rem(c + 1, NC), lax.rem(c + NC - 1, NC)
    c_cross = lax.rem(c + 2 * k - 1 + NC, NC)

    def cid(a, b, d):
        return (a * NZ + b) * 2 + d

    def at(ctx, head, video):
        return {"ctx": ctx, "head": head, "video": video}

    def remote(src, dst, ssem, rsem, dev):
        return pltpu.make_async_remote_copy(
            src_ref=src, dst_ref=dst, send_sem=ssem, recv_sem=rsem,
            device_id=dev, device_id_type=MESH,
        )

    here = at(c, h, v)

    def zpeer(j):
        return lax.rem(z + j, NZ)

    def far_first(fn):
        def step(i):
            half = lax.div(i + 1, 2)
            fn(4 + half - 2 * half * lax.rem(i, 2))

        each(0, NZ - 1, step)

    def ppeer(d):
        return (
            lax.rem(xh + lax.div(d, 4), 2),
            lax.rem(k + lax.rem(lax.div(d, 2), 2), 2),
            lax.rem(v + lax.rem(d, 2), 2),
        )

    def bid(a, b, d):
        return a * 4 + b * 2 + d

    barrier = pltpu.get_barrier_semaphore()

    def signal(dev):
        pl.semaphore_signal(barrier, inc=1, device_id=dev, device_id_type=MESH)

    each(1, NZ, lambda j: signal(at(cid(xh, zpeer(j), k), h, v)))

    def sig_plane(d):
        a, b, e = ppeer(d)
        signal(at(cid(a, z, b), h, e))

    each(1, 8, sig_plane)

    signal(at(c_cross, h, v))
    each(1, NH, lambda j: signal(at(c, lax.rem(h + j, NH), v)))

    own4 = xh * 2 + k
    wrows = pl.ds(pl.multiple_of(h * 896, 128), 896)
    loads = [
        pltpu.make_async_copy(q_ref, qv, lsem.at[0]),
        pltpu.make_async_copy(do_ref, dov, lsem.at[1]),
        pltpu.make_async_copy(k_ref, kb.at[own4], lsem.at[2]),
        pltpu.make_async_copy(v_ref, vb.at[own4], lsem.at[3]),
        pltpu.make_async_copy(w_ref.at[wrows], wb.at[h], lsem.at[4]),
    ]
    for load in loads:
        load.start()
    loads[0].wait()
    loads[1].wait()
    pad = jnp.zeros((8, HD), F32)
    for side, ref in ((0, qv), (1, dov)):
        rows = ref[...].astype(F32)
        parts = [rows[:, g * HD : (g + 1) * HD] for g in range(QPG)] + [pad]
        qg[z, side] = jnp.concatenate(parts, axis=0).astype(BF16)

    row = lax.broadcasted_iota(jnp.int32, (1024, 896), 0)
    col = lax.broadcasted_iota(jnp.int32, (1024, 896), 1)
    inner_row = lax.rem(row, 256)
    quarter = lax.div(row, 256)
    step_of = (
        (inner_row >= PIECE).astype(jnp.int32)
        + (inner_row >= 2 * PIECE).astype(jnp.int32)
        + (inner_row >= 3 * PIECE).astype(jnp.int32)
    )
    source = step_of * (4 * PIECE) + quarter * PIECE + inner_row - step_of * PIECE
    pick = jnp.where((col == source) & (inner_row < 4 * PIECE), 1.0, 0.0).astype(BF16)

    pl.semaphore_wait(barrier, 18)

    def q_copy(j):
        zd = zpeer(j)
        return remote(qg.at[z], qg.at[z], q_s.at[zd], q_r.at[z], at(cid(xh, zd, k), h, v))

    far_first(lambda j: q_copy(j).start())

    def kv_peer(d):
        return lax.rem(xh + lax.div(d, 2), 2), lax.rem(k + lax.rem(d, 2), 2)

    def kv_copy(d, side):
        a, b = kv_peer(d)
        src, dst = ((k_ref, kb), (v_ref, vb))[side]
        return remote(
            src, dst.at[own4], kv_s.at[side, a * 2 + b], kv_r.at[side, own4], at(cid(a, z, b), h, v)
        )

    for side in (0, 1):
        each(1, 4, lambda d: kv_copy(d, side).start())

    def cand_copy(side):
        slot, ctx = ((ko, cid(xh, z, ko)), (k, c_cross))[side]
        rows = pl.ds(pl.multiple_of(slot * BLK + h * 32, 32), 32)
        return remote(enc_ref.at[rows], cand.at[side], c_s.at[side], c_r.at[side], at(ctx, h, v))

    cand_copy(0).start()
    cand_copy(1).start()

    half_rows = pl.ds(pl.multiple_of(k * 448, 64), 448)
    rest_rows = pl.ds(pl.multiple_of(ko * 448, 64), 448)

    def w_copy(j):
        hd = lax.rem(h + j, NH)
        rows = pl.ds(pl.multiple_of(hd * 896 + k * 448, 64), 448)
        return remote(w_ref.at[rows], wb.at[h, half_rows], w_s.at[hd], w_r.at[h], at(c, hd, v))

    def w_forward(j):
        hs = lax.rem(h + j, NH)
        part = wb.at[hs, half_rows]
        remote(part, part, w_s.at[hs], w_r.at[hs], here).wait_recv()
        w_pass(j).start()

    def w_pass(j):
        hs = lax.rem(h + j, NH)
        part = wb.at[hs, half_rows]
        return remote(part, part, wf_s.at[hs], wf_r.at[hs], at(cid(xh, z, ko), h, v))

    def w_arrived(j):
        hs = lax.rem(h + j, NH)
        part = wb.at[hs, rest_rows]
        remote(part, part, wf_s.at[hs], wf_r.at[hs], here).wait_recv()

    each(1, NH, lambda j: w_copy(j).start())

    def q_arrived(j):
        zs = zpeer(j)
        remote(qg.at[zs], qg.at[zs], q_s.at[zs], q_r.at[zs], here).wait_recv()

    def kv_arrived(d):
        a, b = kv_peer(d)
        i = a * 2 + b
        remote(k_ref, kb.at[i], kv_s.at[0, i], kv_r.at[0, i], here).wait_recv()
        remote(v_ref, vb.at[i], kv_s.at[1, i], kv_r.at[1, i], here).wait_recv()

    loads[2].wait()
    loads[3].wait()
    each(1, 4, kv_arrived)
    each(1, NZ, q_arrived)
    keys = kb[...].reshape(512, HD)
    queries = qg[:, 0].reshape(512, HD)
    dout = qg[:, 1].reshape(512, HD)
    block = lax.div(lax.broadcasted_iota(jnp.int32, (512, 512), 0), BLK)
    place = lax.div(block, 2) * (2 * NZ) + z * 2 + lax.rem(block, 2)
    valid = place < len_ref[0]
    masked = jnp.where(valid, nt(keys, queries) * factor, -1e30)
    top = jnp.max(masked, axis=0, keepdims=True)
    terms = jnp.where(valid, jnp.exp(masked - top), 0.0)
    grad_prob = nt(vb[...].reshape(512, HD), dout)
    es[...] = terms
    dp[...] = grad_prob
    total = jnp.sum(terms, axis=0, keepdims=True)
    inner = jnp.sum(terms * grad_prob, axis=0, keepdims=True)
    for n, value in enumerate((top, total, inner)):
        for t in range(4):
            st[z, n * 4 + t : n * 4 + t + 1, :] = value[:, t * 128 : (t + 1) * 128]

    def st_copy(j):
        zd = zpeer(j)
        return remote(st.at[z], st.at[z], st_s.at[zd], st_r.at[z], at(cid(xh, zd, k), h, v))

    def st_arrived(j):
        zs = zpeer(j)
        remote(st.at[zs], st.at[zs], st_s.at[zs], st_r.at[zs], here).wait_recv()

    far_first(lambda j: st_copy(j).start())

    owner = own_ref[0, 0]
    b_me = bid(xh, k, v)
    for side in (0, 1):
        cand_copy(side).wait_recv()
    same = jnp.full((32, 3584), owner, jnp.int32) == c + 1 - 2 * k
    chosen = jnp.where(same, cand[0].astype(F32), cand[1].astype(F32)).astype(BF16)
    stacked = jnp.concatenate([chosen[:, g * 896 : (g + 1) * 896] for g in range(4)], axis=0)
    turned = nt(stacked, pick).astype(BF16)
    for g in range(4):
        for t in range(4):
            encs[g // 2, t, :, (g % 2) * 256 : (g % 2) * 256 + 256] = turned[
                g * 32 : (g + 1) * 32, t * 256 : (t + 1) * 256
            ]

    def ex_copy(d):
        a, b, e = ppeer(d)
        return remote(
            encs.at[a, b * 2 + e], encb.at[h, b_me], ex_s.at[d], ex_r.at[b_me],
            at(cid(a, z, b), h, e),
        )

    def ex_arrived(d):
        i = bid(*ppeer(d))
        remote(encb.at[h, i], encb.at[h, i], ex_s.at[d], ex_r.at[i], here).wait_recv()

    def ey_copy(j):
        hd = lax.rem(h + j, NH)
        return remote(encb.at[h], encb.at[h], ey_s.at[hd], ey_r.at[h], at(c, hd, v))

    def ey_arrived(j):
        hs = lax.rem(h + j, NH)
        remote(encb.at[hs], encb.at[hs], ey_s.at[hs], ey_r.at[hs], here).wait_recv()

    each(1, 8, lambda d: ex_copy(d).start())
    encb[h, b_me] = encs[xh, k * 2 + v]
    each(1, NZ, st_arrived)
    tops, totals, inners = st[:, 0:4, :], st[:, 4:8, :], st[:, 8:12, :]
    upper = jnp.max(tops, axis=0)
    scales = jnp.exp(tops - upper[None])
    sum_total = jnp.sum(totals * scales, axis=0)
    sum_inner = jnp.sum(inners * scales, axis=0)
    cs[0:4, :] = jnp.exp(st[z, 0:4, :] - upper) / sum_total
    cs[4:8, :] = sum_inner / sum_total
    scale = jnp.concatenate([cs[t : t + 1, :] for t in range(4)], axis=1)
    ratio = jnp.concatenate([cs[t : t + 1, :] for t in range(4, 8)], axis=1)
    attention = es[...] * scale
    score_low = (attention * (dp[...] - ratio)).astype(BF16)
    attention_low = attention.astype(BF16)
    key_grad = jnp.dot(score_low, queries, preferred_element_type=F32) * factor
    value_grad = jnp.dot(attention_low, dout, preferred_element_type=F32)
    key_value = jnp.concatenate([key_grad, value_grad], axis=1).reshape(4, BLK, 256)
    dkvf[...] = key_value
    dkvp[...] = key_value.astype(BF16)

    def rs_copy(d):
        a, b = kv_peer(d)
        i = a * 2 + b
        return remote(dkvp.at[i], dkvr.at[own4], rs_s.at[i], rs_r.at[own4], at(cid(a, z, b), h, v))

    def rs_arrived(d):
        a, b = kv_peer(d)
        i = a * 2 + b
        remote(dkvp.at[i], dkvr.at[i], rs_s.at[i], rs_r.at[i], here).wait_recv()

    each(1, 4, lambda d: rs_copy(d).start())

    dqp[...] = tn(score_low, keys).reshape(NZ, 64, HD).astype(BF16)

    def dq_copy(j):
        zd = zpeer(j)
        return remote(dqp.at[zd], dqr.at[z], dq_s.at[zd], dq_r.at[z], at(cid(xh, zd, k), h, v))

    def dq_arrived(j):
        zs = zpeer(j)
        remote(dqp.at[zs], dqr.at[zs], dq_s.at[zs], dq_r.at[zs], here).wait_recv()

    far_first(lambda j: dq_copy(j).start())
    each(1, 8, ex_arrived)
    each(1, NH, lambda j: ey_copy(j).start())
    each(1, NH, w_forward)
    each(1, 4, rs_arrived)
    mine = dkvf[own4]
    for d in range(1, 4):
        a, b = kv_peer(d)
        mine = mine + dkvr[a * 2 + b].astype(F32)
    mine = mine.astype(BF16)
    dkvg[b_me] = mine
    hg[h] = mine

    def gx_peer(d):
        return lax.rem(xh + lax.div(d, 2), 2), lax.rem(v + lax.rem(d, 2), 2)

    def gx_copy(d):
        a, e = gx_peer(d)
        return remote(
            dkvg.at[b_me], dkvg.at[b_me], gx_s.at[a * 2 + e], gx_r.at[xh * 2 + v],
            at(cid(a, z, k), h, e),
        )

    def gc_copy(d):
        a, e = gx_peer(d)
        i = bid(a, k, e)
        return remote(
            dkvg.at[i], dkvg.at[i], gc_s.at[a * 2 + e], gc_r.at[a * 2 + e], at(cid(xh, z, ko), h, v)
        )

    def h_copy(j):
        hd = lax.rem(h + j, NH)
        return remote(hg.at[h], hg.at[h], h_s.at[hd], h_r.at[h], at(c, hd, v))

    each(1, 4, lambda d: gx_copy(d).start())
    each(1, NH, lambda j: h_copy(j).start())
    gc_copy(0).start()

    def forward(d):
        a, e = gx_peer(d)
        i = bid(a, k, e)
        remote(
            dkvg.at[i], dkvg.at[i], gx_s.at[a * 2 + e], gx_r.at[a * 2 + e], here
        ).wait_recv()
        gc_copy(d).start()

    each(1, 4, forward)

    def gc_arrived(d):
        a, e = gx_peer(d)
        i = bid(a, ko, e)
        remote(dkvg.at[i], dkvg.at[i], gc_s.at[a * 2 + e], gc_r.at[a * 2 + e], here).wait_recv()

    each(0, 4, gc_arrived)
    each(1, NH, ey_arrived)
    grads = jnp.concatenate(
        [dkvg[i, n * 32 : (n + 1) * 32, :] for n in range(NH) for i in range(8)], axis=0
    )
    acc = tn(encb[...].reshape(1024, 512), grads)
    for t in range(NZ):
        first = (t // 4) * 256 + (t % 4) * PIECE
        wgs[t] = acc[first : first + 64].astype(BF16)

    def wg_copy(j):
        zd = zpeer(j)
        return remote(wgs.at[zd], wgr.at[z], wg_s.at[zd], wg_r.at[z], at(cid(xh, zd, k), h, v))

    def wg_arrived(j):
        zs = zpeer(j)
        remote(wgs.at[zs], wgr.at[zs], wg_s.at[zs], wg_r.at[zs], here).wait_recv()

    far_first(lambda j: wg_copy(j).start())

    def h_arrived(j):
        hs = lax.rem(h + j, NH)
        remote(hg.at[hs], hg.at[hs], h_s.at[hs], h_r.at[hs], here).wait_recv()

    loads[4].wait()
    each(1, NH, w_arrived)
    each(1, NH, h_arrived)
    summed = jnp.zeros((BLK, 896), F32)
    for g in range(NH):
        summed = summed + nt(hg[g], wb[g]).astype(BF16).astype(F32)
    owners = jnp.full((BLK, 896), owner, jnp.int32)
    egs[0] = jnp.where(owners == c_next, summed, 0.0).astype(BF16)
    egs[1] = jnp.where(owners == c_next, 0.0, summed).astype(BF16)
    out_next = remote(
        egs.at[0], eg_ref.at[pl.ds(0, 128)], o_s.at[0], o_r.at[0], at(c_next, h, v)
    )
    out_prev = remote(
        egs.at[1], eg_ref.at[pl.ds(128, 128)], o_s.at[1], o_r.at[1], at(c_prev, h, v)
    )
    out_next.start()
    out_prev.start()

    each(1, NZ, dq_arrived)
    query_grad = dqp[z].astype(F32)
    for j in range(1, NZ):
        query_grad = query_grad + dqr[zpeer(j)].astype(F32)
    query_grad = query_grad * factor
    dq_ref[...] = jnp.concatenate(
        [query_grad[g * 8 : (g + 1) * 8] for g in range(QPG)], axis=1
    ).astype(BF16)

    each(1, NZ, lambda j: q_copy(j).wait_send())
    for side in (0, 1):
        each(1, 4, lambda d: kv_copy(d, side).wait_send())
    for side in (0, 1):
        cand_copy(side).wait_send()
    each(1, NH, lambda j: w_copy(j).wait_send())
    each(1, NH, lambda j: w_pass(j).wait_send())
    each(1, 8, lambda d: ex_copy(d).wait_send())
    each(1, NH, lambda j: ey_copy(j).wait_send())
    each(1, NZ, lambda j: st_copy(j).wait_send())
    each(1, 4, lambda d: rs_copy(d).wait_send())
    each(1, NZ, lambda j: dq_copy(j).wait_send())
    each(1, 4, lambda d: gx_copy(d).wait_send())
    each(0, 4, lambda d: gc_copy(d).wait_send())
    each(1, NH, lambda j: h_copy(j).wait_send())

    each(1, NZ, wg_arrived)
    weight = wgs[z].astype(F32)
    for j in range(1, NZ):
        weight = weight + wgr[zpeer(j)].astype(F32)
    wg_ref[...] = weight[:PIECE]

    out_next.wait_recv()
    out_prev.wait_recv()
    out_next.wait_send()
    out_prev.wait_send()
    each(1, NZ, lambda j: wg_copy(j).wait_send())


def per_device(queries, keys, values, dout, lengths, owner, enc_rows, w_kv):
    dma = pltpu.SemaphoreType.DMA
    vmem = pltpu.VMEM
    hbm = pl.BlockSpec(memory_space=pl.ANY)
    smem = pl.BlockSpec(memory_space=pltpu.SMEM)
    out = pl.BlockSpec(memory_space=pltpu.VMEM)
    dq, eg, wg = pl.pallas_call(
        kernel,
        out_shape=(
            jax.ShapeDtypeStruct((8, 896), BF16),
            jax.ShapeDtypeStruct((256, 896), BF16),
            jax.ShapeDtypeStruct((PIECE, 256), F32),
        ),
        in_specs=[hbm, hbm, hbm, hbm, smem, smem, hbm, hbm],
        out_specs=(out, hbm, out),
        scratch_shapes=[
            vmem((8, 896), BF16),
            vmem((8, 896), BF16),
            vmem((NZ, 2, 64, HD), BF16),
            vmem((4, BLK, HD), BF16),
            vmem((4, BLK, HD), BF16),
            vmem((2, 32, 3584), BF16),
            vmem((2, 4, 32, 512), BF16),
            vmem((NH, 8, 32, 512), BF16),
            vmem((NH, 896, 256), BF16),
            vmem((NZ, 16, 128), F32),
            vmem((8, 128), F32),
            vmem((512, 512), F32),
            vmem((512, 512), F32),
            vmem((4, BLK, 256), BF16),
            vmem((4, BLK, 256), BF16),
            vmem((4, BLK, 256), F32),
            vmem((8, BLK, 256), BF16),
            vmem((NH, BLK, 256), BF16),
            vmem((NZ, 64, HD), BF16),
            vmem((NZ, 64, HD), BF16),
            vmem((2, BLK, 896), BF16),
            vmem((NZ, 64, 256), BF16),
            vmem((NZ, 64, 256), BF16),
            dma((5,)),
            dma((NZ,)), dma((NZ,)),
            dma((2, 4)), dma((2, 4)),
            dma((NZ,)), dma((NZ,)),
            dma((NZ,)), dma((NZ,)),
            dma((4,)), dma((4,)),
            dma((4,)), dma((4,)),
            dma((4,)), dma((4,)),
            dma((2,)), dma((2,)),
            dma((8,)), dma((8,)),
            dma((NH,)), dma((NH,)),
            dma((NH,)), dma((NH,)),
            dma((NH,)), dma((NH,)),
            dma((NH,)), dma((NH,)),
            dma((2,)), dma((2,)),
            dma((NZ,)), dma((NZ,)),
        ],
        compiler_params=pltpu.CompilerParams(
            collective_id=0, has_side_effects=True, vmem_limit_bytes=60 * 1024 * 1024
        ),
    )(queries[0], keys[0], values[0], dout[0], lengths, owner, enc_rows[0], w_kv)
    return dq[None], eg[None], wg


def solution(mesh):
    placed = (
        P("video", "ctx", "head"),
        P("video", "ctx", "head"),
        P("video", "ctx", "head"),
        P("video", "ctx", "head"),
        P("video"),
        P("video", "ctx"),
        P("video", "ctx", None),
        P(None, "head"),
    )
    return jax.shard_map(
        per_device,
        mesh=mesh,
        in_specs=placed,
        out_specs=(
            P("video", "ctx", "head"),
            P("video", "ctx", "head"),
            P(("ctx", "video"), "head"),
        ),
        check_vma=False,
    )
```

```python
import math

import jax
import jax.numpy as jnp
from jax import lax
from jax.experimental import pallas as pl
from jax.experimental.pallas import tpu as pltpu
from jax.sharding import PartitionSpec as P

NZ = 8
NC = 32
NH = 4
HD = 128
BLK = 128
QPG = 7
PIECE = 56
F32 = jnp.float32
BF16 = jnp.bfloat16
MESH = pl.DeviceIdType.MESH


def each(start, stop, fn):
    def step(i, carry):
        fn(i)
        return carry

    lax.fori_loop(start, stop, step, 0)


def nt(a, b):
    return lax.dot_general(a, b, (((1,), (1,)), ((), ())), preferred_element_type=F32)


def tn(a, b):
    return lax.dot_general(a, b, (((0,), (0,)), ((), ())), preferred_element_type=F32)


def kernel(
    q_ref, k_ref, v_ref, do_ref, len_in, own_in, enc_ref, w_ref,
    dq_ref, eg_ref, wg_ref,
    len_ref, own_ref, qv, dov, qg, kb, vb, cand, encs, encb, wb, st, cs, es, dp,
    dkvp, dkvr, dkvf, dkvg, hg, dqp, dqr, egs, wgs, wgr,
    lsem, q_s, q_r, kv_s, kv_r, st_s, st_r, dq_s, dq_r, rs_s, rs_r,
    gx_s, gx_r, gc_s, gc_r, c_s, c_r, ex_s, ex_r, ey_s, ey_r,
    w_s, w_r, wf_s, wf_r, h_s, h_r, o_s, o_r, wg_s, wg_r,
):
    factor = 1.0 / math.sqrt(HD)
    c = lax.axis_index("ctx")
    h = lax.axis_index("head")
    v = lax.axis_index("video")
    xh, z, k = lax.div(c, 2 * NZ), lax.rem(lax.div(c, 2), NZ), lax.rem(c, 2)
    ko = 1 - k
    c_next, c_prev = lax.rem(c + 1, NC), lax.rem(c + NC - 1, NC)
    c_cross = lax.rem(c + 2 * k - 1 + NC, NC)

    def cid(a, b, d):
        return (a * NZ + b) * 2 + d

    def at(ctx, head, video):
        return {"ctx": ctx, "head": head, "video": video}

    def remote(src, dst, ssem, rsem, dev):
        return pltpu.make_async_remote_copy(
            src_ref=src, dst_ref=dst, send_sem=ssem, recv_sem=rsem,
            device_id=dev, device_id_type=MESH,
        )

    here = at(c, h, v)

    def zpeer(j):
        return lax.rem(z + j, NZ)

    def far_first(fn):
        def step(i):
            half = lax.div(i + 1, 2)
            fn(4 + half - 2 * half * lax.rem(i, 2))

        each(0, NZ - 1, step)

    def ppeer(d):
        return (
            lax.rem(xh + lax.div(d, 4), 2),
            lax.rem(k + lax.rem(lax.div(d, 2), 2), 2),
            lax.rem(v + lax.rem(d, 2), 2),
        )

    def bid(a, b, d):
        return a * 4 + b * 2 + d

    barrier = pltpu.get_barrier_semaphore()

    def signal(dev):
        pl.semaphore_signal(barrier, inc=1, device_id=dev, device_id_type=MESH)

    each(1, NZ, lambda j: signal(at(cid(xh, zpeer(j), k), h, v)))

    def sig_plane(d):
        a, b, e = ppeer(d)
        signal(at(cid(a, z, b), h, e))

    each(1, 8, sig_plane)

    signal(at(c_cross, h, v))
    each(1, NH, lambda j: signal(at(c, lax.rem(h + j, NH), v)))

    own4 = xh * 2 + k
    wrows = pl.ds(pl.multiple_of(h * 896, 128), 896)
    loads = [
        pltpu.make_async_copy(q_ref, qv, lsem.at[0]),
        pltpu.make_async_copy(do_ref, dov, lsem.at[1]),
        pltpu.make_async_copy(k_ref, kb.at[own4], lsem.at[2]),
        pltpu.make_async_copy(v_ref, vb.at[own4], lsem.at[3]),
        pltpu.make_async_copy(w_ref.at[wrows], wb.at[h], lsem.at[4]),
        pltpu.make_async_copy(len_in, len_ref, lsem.at[5]),
        pltpu.make_async_copy(own_in, own_ref, lsem.at[6]),
    ]
    for load in loads:
        load.start()
    loads[0].wait()
    loads[1].wait()
    parts = []
    for ref in (qv, dov):
        rows = ref[...].astype(F32)
        parts += [rows[:, g * HD : (g + 1) * HD] for g in range(QPG)]
    qg[z] = jnp.concatenate(parts, axis=0).astype(BF16)

    pl.semaphore_wait(barrier, 18)

    def q_copy(j):
        zd = zpeer(j)
        return remote(qg.at[z], qg.at[z], q_s.at[zd], q_r.at[z], at(cid(xh, zd, k), h, v))

    far_first(lambda j: q_copy(j).start())

    def kv_peer(d):
        return lax.rem(xh + lax.div(d, 2), 2), lax.rem(k + lax.rem(d, 2), 2)

    def kv_copy(d, side):
        a, b = kv_peer(d)
        src, dst = ((k_ref, kb), (v_ref, vb))[side]
        return remote(
            src, dst.at[own4], kv_s.at[side, a * 2 + b], kv_r.at[side, own4], at(cid(a, z, b), h, v)
        )

    for side in (0, 1):
        each(1, 4, lambda d: kv_copy(d, side).start())

    def cand_copy(side):
        slot, ctx = ((ko, cid(xh, z, ko)), (k, c_cross))[side]
        rows = pl.ds(pl.multiple_of(slot * BLK + h * 32, 32), 32)
        return remote(enc_ref.at[rows], cand.at[side], c_s.at[side], c_r.at[side], at(ctx, h, v))

    cand_copy(0).start()
    cand_copy(1).start()

    half_rows = pl.ds(pl.multiple_of(k * 448, 64), 448)
    rest_rows = pl.ds(pl.multiple_of(ko * 448, 64), 448)

    def w_copy(j):
        hd = lax.rem(h + j, NH)
        rows = pl.ds(pl.multiple_of(hd * 896 + k * 448, 64), 448)
        return remote(w_ref.at[rows], wb.at[h, half_rows], w_s.at[hd], w_r.at[h], at(c, hd, v))

    def w_forward(j):
        hs = lax.rem(h + j, NH)
        part = wb.at[hs, half_rows]
        remote(part, part, w_s.at[hs], w_r.at[hs], here).wait_recv()
        w_pass(j).start()

    def w_pass(j):
        hs = lax.rem(h + j, NH)
        part = wb.at[hs, half_rows]
        return remote(part, part, wf_s.at[hs], wf_r.at[hs], at(cid(xh, z, ko), h, v))

    def w_arrived(j):
        hs = lax.rem(h + j, NH)
        part = wb.at[hs, rest_rows]
        remote(part, part, wf_s.at[hs], wf_r.at[hs], here).wait_recv()

    each(1, NH, lambda j: w_copy(j).start())

    def q_arrived(j):
        zs = zpeer(j)
        remote(qg.at[zs], qg.at[zs], q_s.at[zs], q_r.at[zs], here).wait_recv()

    def kv_arrived(d):
        a, b = kv_peer(d)
        i = a * 2 + b
        remote(k_ref, kb.at[i], kv_s.at[0, i], kv_r.at[0, i], here).wait_recv()
        remote(v_ref, vb.at[i], kv_s.at[1, i], kv_r.at[1, i], here).wait_recv()

    loads[2].wait()
    loads[3].wait()
    loads[5].wait()
    loads[6].wait()
    each(1, 4, kv_arrived)
    each(1, NZ, q_arrived)
    keys = kb[...].reshape(512, HD)
    text = qg[...].astype(F32)
    rest = jnp.zeros((512 - NZ * PIECE, HD), F32)

    def text_rows(first):
        rows = text[:, first : first + PIECE].reshape(NZ * PIECE, HD)
        return jnp.concatenate([rows, rest], axis=0).astype(BF16)

    queries, dout = text_rows(0), text_rows(PIECE)
    block = lax.div(lax.broadcasted_iota(jnp.int32, (512, 512), 0), BLK)
    place = lax.div(block, 2) * (2 * NZ) + z * 2 + lax.rem(block, 2)
    valid = place < len_ref[0]
    masked = jnp.where(valid, nt(keys, queries) * factor, -1e30)
    top = jnp.max(masked, axis=0, keepdims=True)
    terms = jnp.where(valid, jnp.exp(masked - top), 0.0)
    grad_prob = nt(vb[...].reshape(512, HD), dout)
    es[...] = terms
    dp[...] = grad_prob
    total = jnp.sum(terms, axis=0, keepdims=True)
    inner = jnp.sum(terms * grad_prob, axis=0, keepdims=True)
    for n, value in enumerate((top, total, inner)):
        for t in range(4):
            st[z, n * 4 + t : n * 4 + t + 1, :] = value[:, t * 128 : (t + 1) * 128]

    def st_copy(j):
        zd = zpeer(j)
        return remote(st.at[z], st.at[z], st_s.at[zd], st_r.at[z], at(cid(xh, zd, k), h, v))

    def st_arrived(j):
        zs = zpeer(j)
        remote(st.at[zs], st.at[zs], st_s.at[zs], st_r.at[zs], here).wait_recv()

    far_first(lambda j: st_copy(j).start())

    owner = own_ref[0, 0]
    b_me = bid(xh, k, v)
    cand_copy(0).wait_recv()
    cand_copy(1).wait_recv()
    same = jnp.full((32, 3584), owner, jnp.int32) == c + 1 - 2 * k
    chosen = jnp.where(same, cand[0].astype(F32), cand[1].astype(F32))
    blank = jnp.zeros((32, 512 - NZ * PIECE), F32)
    for a in (0, 1):
        for t in range(4):
            starts = [a * 1792 + n * 4 * PIECE + t * PIECE for n in range(NZ)]
            pieces = [chosen[:, first : first + PIECE] for first in starts]
            encs[a, t] = jnp.concatenate(pieces + [blank], axis=1).astype(BF16)

    def ex_copy(d):
        a, b, e = ppeer(d)
        return remote(
            encs.at[a, b * 2 + e], encb.at[h, b_me], ex_s.at[d], ex_r.at[b_me],
            at(cid(a, z, b), h, e),
        )

    def ex_arrived(d):
        i = bid(*ppeer(d))
        remote(encb.at[h, i], encb.at[h, i], ex_s.at[d], ex_r.at[i], here).wait_recv()

    up, down, far = lax.rem(h + 1, NH), lax.rem(h + 3, NH), lax.rem(h + 2, NH)

    def ey_copy(side):
        hd = (up, down)[side]
        return remote(encb.at[h], encb.at[h], ey_s.at[side], ey_r.at[side], at(c, hd, v))

    def ey_arrived(side):
        hs = (down, up)[side]
        remote(encb.at[hs], encb.at[hs], ey_s.at[side], ey_r.at[side], here).wait_recv()

    def ey_pass(side):
        part = encb.at[(down, up)[side], pl.ds(4 * side, 4)]
        return remote(part, part, ey_s.at[2 + side], ey_r.at[2 + side], at(c, (up, down)[side], v))

    def ey_passed(side):
        part = encb.at[far, pl.ds(4 * side, 4)]
        remote(part, part, ey_s.at[2 + side], ey_r.at[2 + side], here).wait_recv()

    each(1, 8, lambda d: ex_copy(d).start())
    encb[h, b_me] = encs[xh, k * 2 + v]
    each(1, NZ, st_arrived)
    tops, totals, inners = st[:, 0:4, :], st[:, 4:8, :], st[:, 8:12, :]
    upper = jnp.max(tops, axis=0)
    scales = jnp.exp(tops - upper[None])
    sum_total = jnp.sum(totals * scales, axis=0)
    sum_inner = jnp.sum(inners * scales, axis=0)
    cs[0:4, :] = jnp.exp(st[z, 0:4, :] - upper) / sum_total
    cs[4:8, :] = sum_inner / sum_total
    scale = jnp.concatenate([cs[t : t + 1, :] for t in range(4)], axis=1)
    ratio = jnp.concatenate([cs[t : t + 1, :] for t in range(4, 8)], axis=1)
    attention = es[...] * scale
    score_low = (attention * (dp[...] - ratio)).astype(BF16)
    attention_low = attention.astype(BF16)
    key_grad = jnp.dot(score_low, queries, preferred_element_type=F32) * factor
    value_grad = jnp.dot(attention_low, dout, preferred_element_type=F32)
    key_value = jnp.concatenate([key_grad, value_grad], axis=1).reshape(4, BLK, 256)
    dkvf[...] = key_value
    dkvp[...] = key_value.astype(BF16)

    def rs_copy(d):
        a, b = kv_peer(d)
        i = a * 2 + b
        return remote(dkvp.at[i], dkvr.at[own4], rs_s.at[i], rs_r.at[own4], at(cid(a, z, b), h, v))

    def rs_arrived(d):
        a, b = kv_peer(d)
        i = a * 2 + b
        remote(dkvp.at[i], dkvr.at[i], rs_s.at[i], rs_r.at[i], here).wait_recv()

    each(1, 4, lambda d: rs_copy(d).start())

    query_part = tn(score_low, keys)
    for t in range(NZ):
        dqp[t] = query_part[t * PIECE : t * PIECE + 64].astype(BF16)

    def dq_copy(j):
        zd = zpeer(j)
        return remote(dqp.at[zd], dqr.at[z], dq_s.at[zd], dq_r.at[z], at(cid(xh, zd, k), h, v))

    def dq_arrived(j):
        zs = zpeer(j)
        remote(dqp.at[zs], dqr.at[zs], dq_s.at[zs], dq_r.at[zs], here).wait_recv()

    far_first(lambda j: dq_copy(j).start())
    each(1, 8, ex_arrived)
    ey_copy(0).start()
    ey_copy(1).start()
    each(1, NH, w_forward)
    each(1, 4, rs_arrived)
    mine = dkvf[own4]
    for d in range(1, 4):
        a, b = kv_peer(d)
        mine = mine + dkvr[a * 2 + b].astype(F32)
    mine = mine.astype(BF16)
    dkvg[b_me] = mine
    hg[h] = mine

    def gx_peer(d):
        return lax.rem(xh + lax.div(d, 2), 2), lax.rem(v + lax.rem(d, 2), 2)

    def gx_copy(d):
        a, e = gx_peer(d)
        return remote(
            dkvg.at[b_me], dkvg.at[b_me], gx_s.at[a * 2 + e], gx_r.at[xh * 2 + v],
            at(cid(a, z, k), h, e),
        )

    def gc_copy(d):
        a, e = gx_peer(d)
        i = bid(a, k, e)
        return remote(
            dkvg.at[i], dkvg.at[i], gc_s.at[a * 2 + e], gc_r.at[a * 2 + e], at(cid(xh, z, ko), h, v)
        )

    def h_copy(j):
        hd = lax.rem(h + j, NH)
        return remote(hg.at[h], hg.at[h], h_s.at[hd], h_r.at[h], at(c, hd, v))

    each(1, 4, lambda d: gx_copy(d).start())
    each(1, NH, lambda j: h_copy(j).start())
    gc_copy(0).start()

    def forward(d):
        a, e = gx_peer(d)
        i = bid(a, k, e)
        remote(
            dkvg.at[i], dkvg.at[i], gx_s.at[a * 2 + e], gx_r.at[a * 2 + e], here
        ).wait_recv()
        gc_copy(d).start()

    ey_arrived(0)
    ey_pass(0).start()
    ey_arrived(1)
    ey_pass(1).start()
    each(1, 4, forward)

    def h_arrived(j):
        hs = lax.rem(h + j, NH)
        remote(hg.at[hs], hg.at[hs], h_s.at[hs], h_r.at[hs], here).wait_recv()

    loads[4].wait()
    each(1, NH, w_arrived)
    each(1, NH, h_arrived)
    summed = jnp.zeros((BLK, 896), F32)
    for g in range(NH):
        summed = summed + nt(hg[g], wb[g]).astype(BF16).astype(F32)
    owners = jnp.full((BLK, 896), owner, jnp.int32)
    egs[0] = jnp.where(owners == c_next, summed, 0.0).astype(BF16)
    egs[1] = jnp.where(owners == c_next, 0.0, summed).astype(BF16)
    out_next = remote(
        egs.at[0], eg_ref.at[pl.ds(0, 128)], o_s.at[0], o_r.at[0], at(c_next, h, v)
    )
    out_prev = remote(
        egs.at[1], eg_ref.at[pl.ds(128, 128)], o_s.at[1], o_r.at[1], at(c_prev, h, v)
    )
    out_next.start()
    out_prev.start()

    def gc_arrived(d):
        a, e = gx_peer(d)
        i = bid(a, ko, e)
        remote(dkvg.at[i], dkvg.at[i], gc_s.at[a * 2 + e], gc_r.at[a * 2 + e], here).wait_recv()

    each(0, 4, gc_arrived)
    ey_passed(0)
    ey_passed(1)
    grads = jnp.concatenate(
        [dkvg[i, n * 32 : (n + 1) * 32, :] for n in range(NH) for i in range(8)], axis=0
    )
    acc = tn(encb[...].reshape(1024, 512), grads)
    for t in range(NZ):
        piece = acc[t * PIECE : (t + 1) * PIECE]
        wgs[t] = jnp.concatenate([piece[:, :128], piece[:, 128:]], axis=0).astype(BF16)

    def wg_copy(j):
        zd = zpeer(j)
        return remote(wgs.at[zd], wgr.at[z], wg_s.at[zd], wg_r.at[z], at(cid(xh, zd, k), h, v))

    def wg_arrived(j):
        zs = zpeer(j)
        remote(wgs.at[zs], wgr.at[zs], wg_s.at[zs], wg_r.at[zs], here).wait_recv()

    far_first(lambda j: wg_copy(j).start())

    each(1, NZ, dq_arrived)
    query_grad = dqp[z].astype(F32)
    for j in range(1, NZ):
        query_grad = query_grad + dqr[zpeer(j)].astype(F32)
    query_grad = query_grad * factor
    dq_ref[...] = jnp.concatenate(
        [query_grad[g * 8 : (g + 1) * 8] for g in range(QPG)], axis=1
    ).astype(BF16)

    each(1, NZ, lambda j: q_copy(j).wait_send())
    for side in (0, 1):
        each(1, 4, lambda d: kv_copy(d, side).wait_send())
    for side in (0, 1):
        cand_copy(side).wait_send()
    each(1, NH, lambda j: w_copy(j).wait_send())
    each(1, NH, lambda j: w_pass(j).wait_send())
    each(1, 8, lambda d: ex_copy(d).wait_send())
    for side in (0, 1):
        ey_copy(side).wait_send()
        ey_pass(side).wait_send()
    each(1, NZ, lambda j: st_copy(j).wait_send())
    each(1, 4, lambda d: rs_copy(d).wait_send())
    each(1, NZ, lambda j: dq_copy(j).wait_send())
    each(1, 4, lambda d: gx_copy(d).wait_send())
    each(0, 4, lambda d: gc_copy(d).wait_send())
    each(1, NH, lambda j: h_copy(j).wait_send())

    each(1, NZ, wg_arrived)
    weight = wgs[z].astype(F32)
    for j in range(1, NZ):
        weight = weight + wgr[zpeer(j)].astype(F32)
    wg_ref[...] = jnp.concatenate([weight[:PIECE], weight[PIECE:]], axis=1)

    out_next.wait_recv()
    out_prev.wait_recv()
    out_next.wait_send()
    out_prev.wait_send()
    each(1, NZ, lambda j: wg_copy(j).wait_send())


def copy_kernel(dq_in, eg_in, wg_in, dq_out, eg_out, wg_out, sems):
    pairs = ((dq_in, dq_out), (eg_in, eg_out), (wg_in, wg_out))
    moves = [pltpu.make_async_copy(a, b, sems.at[i]) for i, (a, b) in enumerate(pairs)]
    for move in moves:
        move.start()
    for move in moves:
        move.wait()


def finish(dq, eg, wg):
    hbm = pl.BlockSpec(memory_space=pl.ANY)
    arrays = tuple(pltpu.with_memory_space_constraint(a, pltpu.VMEM) for a in (dq, eg, wg))
    outs = pl.pallas_call(
        copy_kernel,
        out_shape=tuple(jax.ShapeDtypeStruct(a.shape, a.dtype) for a in arrays),
        in_specs=[pl.BlockSpec(memory_space=pltpu.VMEM)] * 3,
        out_specs=(hbm,) * 3,
        scratch_shapes=[pltpu.SemaphoreType.DMA((3,))],
    )(*arrays)
    return outs[0][None], outs[1][None], outs[2]


def per_device(queries, keys, values, dout, lengths, owner, enc_rows, w_kv):
    dma = pltpu.SemaphoreType.DMA
    vmem = pltpu.VMEM
    hbm = pl.BlockSpec(memory_space=pl.ANY)
    out = pl.BlockSpec(memory_space=pltpu.VMEM)
    dq, eg, wg = pl.pallas_call(
        kernel,
        out_shape=(
            vmem((8, 896), BF16),
            vmem((256, 896), BF16),
            vmem((PIECE, 256), F32),
        ),
        in_specs=[hbm] * 8,
        out_specs=(out, out, out),
        scratch_shapes=[
            pltpu.SMEM((1,), jnp.int32),
            pltpu.SMEM((1, 1), jnp.int32),
            vmem((8, 896), BF16),
            vmem((8, 896), BF16),
            vmem((NZ, 2 * PIECE, HD), BF16),
            vmem((4, BLK, HD), BF16),
            vmem((4, BLK, HD), BF16),
            vmem((2, 32, 3584), BF16),
            vmem((2, 4, 32, 512), BF16),
            vmem((NH, 8, 32, 512), BF16),
            vmem((NH, 896, 256), BF16),
            vmem((NZ, 16, 128), F32),
            vmem((8, 128), F32),
            vmem((512, 512), F32),
            vmem((512, 512), F32),
            vmem((4, BLK, 256), BF16),
            vmem((4, BLK, 256), BF16),
            vmem((4, BLK, 256), F32),
            vmem((8, BLK, 256), BF16),
            vmem((NH, BLK, 256), BF16),
            vmem((NZ, 64, HD), BF16),
            vmem((NZ, 64, HD), BF16),
            vmem((2, BLK, 896), BF16),
            vmem((NZ, 2 * PIECE, 128), BF16),
            vmem((NZ, 2 * PIECE, 128), BF16),
            dma((7,)),
            dma((NZ,)), dma((NZ,)),
            dma((2, 4)), dma((2, 4)),
            dma((NZ,)), dma((NZ,)),
            dma((NZ,)), dma((NZ,)),
            dma((4,)), dma((4,)),
            dma((4,)), dma((4,)),
            dma((4,)), dma((4,)),
            dma((2,)), dma((2,)),
            dma((8,)), dma((8,)),
            dma((NH,)), dma((NH,)),
            dma((NH,)), dma((NH,)),
            dma((NH,)), dma((NH,)),
            dma((NH,)), dma((NH,)),
            dma((2,)), dma((2,)),
            dma((NZ,)), dma((NZ,)),
        ],
        compiler_params=pltpu.CompilerParams(
            collective_id=0, has_side_effects=True, vmem_limit_bytes=60 * 1024 * 1024
        ),
    )(queries[0], keys[0], values[0], dout[0], lengths, owner, enc_rows[0], w_kv)
    return finish(dq, eg, wg)


def solution(mesh):
    placed = (
        P("video", "ctx", "head"),
        P("video", "ctx", "head"),
        P("video", "ctx", "head"),
        P("video", "ctx", "head"),
        P("video"),
        P("video", "ctx"),
        P("video", "ctx", None),
        P(None, "head"),
    )
    return jax.shard_map(
        per_device,
        mesh=mesh,
        in_specs=placed,
        out_specs=(
            P("video", "ctx", "head"),
            P("video", "ctx", "head"),
            P(("ctx", "video"), "head"),
        ),
        check_vma=False,
    )
```

```python
import math

import jax
import jax.numpy as jnp
from jax import lax
from jax.experimental import pallas as pl
from jax.experimental.pallas import tpu as pltpu
from jax.sharding import PartitionSpec as P

NZ = 8
NC = 32
NH = 4
HD = 128
BLK = 128
QPG = 7
PIECE = 56
F32 = jnp.float32
BF16 = jnp.bfloat16
MESH = pl.DeviceIdType.MESH


SEMS = (
    "q", "k", "w", "small", "q_s", "q_r", "k_s", "k_r", "v_s", "v_r", "st_s", "st_r",
    "dq_s", "dq_r", "rs_s", "rs_r", "gx_s", "gc_s", "gc_r", "c_s", "c_r", "ex_s",
    "eu_s", "ed_s", "ep_s", "ep_r", "w_s", "w_r", "wf_s", "wf_r", "h_s",
    "o_s", "o_r", "wg_s", "wg_r", "do", "v", "own",
)


def each(start, stop, fn):
    def step(i, carry):
        fn(i)
        return carry

    lax.fori_loop(start, stop, step, 0)


def nt(a, b):
    return lax.dot_general(a, b, (((1,), (1,)), ((), ())), preferred_element_type=F32)


def tn(a, b):
    return lax.dot_general(a, b, (((0,), (0,)), ((), ())), preferred_element_type=F32)


def kernel(
    q_ref, k_ref, v_ref, do_ref, len_in, own_in, enc_ref, w_ref,
    dq_ref, eg_ref, wg_ref,
    len_ref, own_ref, qv, dov, qg, kb, vb, cand, encs, encb, wb, st, cs, es, dp,
    dkvp, dkvr, dkvf, dkvg, hg, dqp, dqr, egs, wgs, wgr,
    terms_sum, sems, gx_r, ex_r, ey_r, h_r,
):
    factor = 1.0 / math.sqrt(HD)
    c = lax.axis_index("ctx")
    h = lax.axis_index("head")
    v = lax.axis_index("video")
    xh, z, k = lax.div(c, 2 * NZ), lax.rem(lax.div(c, 2), NZ), lax.rem(c, 2)
    ko = 1 - k
    c_next, c_prev = lax.rem(c + 1, NC), lax.rem(c + NC - 1, NC)
    c_cross = lax.rem(c + 2 * k - 1 + NC, NC)

    def cid(a, b, d):
        return (a * NZ + b) * 2 + d

    def at(ctx, head, video):
        return {"ctx": ctx, "head": head, "video": video}

    def remote(src, dst, ssem, rsem, dev):
        return pltpu.make_async_remote_copy(
            src_ref=src, dst_ref=dst, send_sem=ssem, recv_sem=rsem,
            device_id=dev, device_id_type=MESH,
        )

    here = at(c, h, v)

    def sent(ref, name):
        remote(ref, ref, sem(name + "_s"), sem(name + "_s"), here).wait_send()

    def arrived(ref, name):
        remote(ref, ref, sem(name + "_r"), sem(name + "_r"), here).wait_recv()

    def sem(name):
        return sems.at[SEMS.index(name)]

    def zpeer(j):
        return lax.rem(z + j, NZ)

    def far_first(fn):
        def step(i):
            half = lax.div(i + 1, 2)
            fn(4 + half - 2 * half * lax.rem(i, 2))

        each(0, NZ - 1, step)

    def ppeer(d):
        return (
            lax.rem(xh + lax.div(d, 4), 2),
            lax.rem(k + lax.rem(lax.div(d, 2), 2), 2),
            lax.rem(v + lax.rem(d, 2), 2),
        )

    def bid(a, b, d):
        return a * 4 + d * 2 + b

    barrier = pltpu.get_barrier_semaphore()

    def signal(dev):
        pl.semaphore_signal(barrier, inc=1, device_id=dev, device_id_type=MESH)

    each(1, NZ, lambda j: signal(at(cid(xh, zpeer(j), k), h, v)))

    def sig_plane(d):
        a, b, e = ppeer(d)
        signal(at(cid(a, z, b), h, e))

    each(1, 8, sig_plane)

    signal(at(c_cross, h, v))
    each(1, NH, lambda j: signal(at(c, lax.rem(h + j, NH), v)))

    own4 = xh * 2 + k
    wrows = pl.ds(pl.multiple_of(h * 896, 128), 896)
    loads = [
        pltpu.make_async_copy(q_ref, qv, sem("q")),
        pltpu.make_async_copy(do_ref, dov, sem("do")),
        pltpu.make_async_copy(k_ref, kb.at[own4], sem("k")),
        pltpu.make_async_copy(v_ref, vb.at[own4], sem("v")),
        pltpu.make_async_copy(w_ref.at[wrows], wb.at[wrows], sem("w")),
        pltpu.make_async_copy(len_in, len_ref, sem("small")),
        pltpu.make_async_copy(own_in, own_ref, sem("own")),
    ]
    for load in loads:
        load.start()
    loads[0].wait()
    loads[1].wait()
    parts = []
    for ref in (qv, dov):
        rows = ref[...].astype(F32)
        parts += [rows[:, g * HD : (g + 1) * HD] for g in range(QPG)]
    qg[z] = jnp.concatenate(parts, axis=0).astype(BF16)

    pl.semaphore_wait(barrier, 18)

    def q_copy(j):
        zd = zpeer(j)
        return remote(qg.at[z], qg.at[z], sem("q_s"), sem("q_r"), at(cid(xh, zd, k), h, v))

    far_first(lambda j: q_copy(j).start())

    def kv_peer(d):
        return lax.rem(xh + lax.div(d, 2), 2), lax.rem(k + lax.rem(d, 2), 2)

    def kv_copy(d, side):
        a, b = kv_peer(d)
        src, dst = ((k_ref, kb), (v_ref, vb))[side]
        name = ("k", "v")[side]
        return remote(
            src, dst.at[own4], sem(name + "_s"), sem(name + "_r"), at(cid(a, z, b), h, v)
        )

    for side in (0, 1):
        each(1, 4, lambda d: kv_copy(d, side).start())

    def cand_copy(side):
        slot, ctx = ((ko, cid(xh, z, ko)), (k, c_cross))[side]
        rows = pl.ds(pl.multiple_of(slot * BLK + h * 32, 32), 32)
        return remote(enc_ref.at[rows], cand.at[side], sem("c_s"), sem("c_r"), at(ctx, h, v))

    cand_copy(0).start()
    cand_copy(1).start()

    def w_rows(hd, core):
        return pl.ds(pl.multiple_of(hd * 896 + core * 448, 64), 448)

    def w_copy(j):
        hd = lax.rem(h + j, NH)
        return remote(
            w_ref.at[w_rows(hd, k)], wb.at[w_rows(h, k)], sem("w_s"), sem("w_r"), at(c, hd, v)
        )

    def w_pass(j):
        part = wb.at[w_rows(lax.rem(h + j, NH), k)]
        return remote(part, part, sem("wf_s"), sem("wf_r"), at(cid(xh, z, ko), h, v))

    three_halves = wb.at[pl.ds(0, 3 * 448)]
    each(1, NH, lambda j: w_copy(j).start())

    loads[2].wait()
    loads[3].wait()
    loads[5].wait()
    loads[6].wait()
    arrived(kb.at[pl.ds(0, 3)], "k")
    arrived(vb.at[pl.ds(0, 3)], "v")
    arrived(qg.at[pl.ds(0, 7)], "q")
    keys = kb[...].reshape(512, HD)
    text = qg[...].astype(F32)
    rest = jnp.zeros((512 - NZ * PIECE, HD), F32)

    def text_rows(first):
        rows = text[:, first : first + PIECE].reshape(NZ * PIECE, HD)
        return jnp.concatenate([rows, rest], axis=0).astype(BF16)

    queries, dout = text_rows(0), text_rows(PIECE)
    block = lax.div(lax.broadcasted_iota(jnp.int32, (512, 512), 0), BLK)
    place = lax.div(block, 2) * (2 * NZ) + z * 2 + lax.rem(block, 2)
    valid = place < len_ref[0]
    masked = jnp.where(valid, nt(keys, queries) * factor, -1e30)
    top = jnp.max(masked, axis=0, keepdims=True)
    terms = jnp.where(valid, jnp.exp(masked - top), 0.0)
    grad_prob = nt(vb[...].reshape(512, HD), dout)
    es[...] = terms
    dp[...] = grad_prob
    total = jnp.sum(terms, axis=0, keepdims=True)
    inner = jnp.sum(terms * grad_prob, axis=0, keepdims=True)
    for n, value in enumerate((top, total, inner)):
        for t in range(4):
            st[z, n * 4 + t : n * 4 + t + 1, :] = value[:, t * 128 : (t + 1) * 128]

    def st_copy(j):
        zd = zpeer(j)
        return remote(st.at[z], st.at[z], sem("st_s"), sem("st_r"), at(cid(xh, zd, k), h, v))

    far_first(lambda j: st_copy(j).start())

    owner = own_ref[0, 0]
    b_me = bid(xh, k, v)
    arrived(cand, "c")
    same = jnp.full((32, 3584), owner, jnp.int32) == c + 1 - 2 * k
    chosen = jnp.where(same, cand[0].astype(F32), cand[1].astype(F32))
    for a in (0, 1):
        for t in range(4):
            starts = [a * 1792 + n * 4 * PIECE + t * PIECE for n in range(NZ)]
            pieces = [
                chosen[first : first + 16, start : start + PIECE]
                for first in (0, 16)
                for start in starts
            ]
            encs[a, t] = jnp.concatenate(pieces, axis=1).astype(BF16)

    def ex_copy(d):
        a, b, e = ppeer(d)
        return remote(
            encs.at[a, b * 2 + e], encb.at[h, b_me], sem("ex_s"), ex_r.at[xh * 2 + v],
            at(cid(a, z, b), h, e),
        )

    up, down, far = lax.rem(h + 1, NH), lax.rem(h + 3, NH), lax.rem(h + 2, NH)

    def chip(i):
        return lax.rem(xh + i // 2, 2), lax.rem(v + ((i + 1) // 2) % 2, 2)

    def chunk(hd, i):
        if i < 2:
            return encb.at[hd, pl.ds(bid(xh, (k, ko)[i], v), 1)]
        a, e = chip(i - 1)
        return encb.at[hd, pl.ds(bid(a, 0, e), 2)]

    def ey_copy(side, i):
        part = chunk(h, i)
        return remote(
            part, part, sem(("eu_s", "ed_s")[side]), ey_r.at[side, i], at(c, (up, down)[side], v)
        )

    def ey_arrived(side, i):
        part = chunk((down, up)[side], i)
        remote(part, part, sem("eu_s"), ey_r.at[side, i], here).wait_recv()

    def ey_send(i):
        if i > 0:
            a, e = chip(i - 1)
            part = chunk(h, i)
            remote(part, part, sem("ex_s"), ex_r.at[a * 2 + e], here).wait_recv()
        ey_copy(0, i).start()
        if i not in (1, 2):
            ey_copy(1, i).start()

    def pass_side(i):
        return 0 if i < 3 else 1

    def ey_pass(i):
        side = pass_side(i)
        part = chunk((down, up)[side], i)
        return remote(part, part, sem("ep_s"), sem("ep_r"), at(c, (up, down)[side], v))

    def ey_relay(i):
        ey_arrived(pass_side(i), i)
        ey_pass(i).start()

    encb[h, b_me] = encs[xh, k * 2 + v]
    ey_send(0)
    for d in (2, 1, 3, 5, 7, 4, 6):
        ex_copy(d).start()
    arrived(st.at[pl.ds(0, 7)], "st")
    tops, totals, inners = st[:, 0:4, :], st[:, 4:8, :], st[:, 8:12, :]
    upper = jnp.max(tops, axis=0)
    scales = jnp.exp(tops - upper[None])
    sum_total = jnp.sum(totals * scales, axis=0)
    sum_inner = jnp.sum(inners * scales, axis=0)
    cs[0:4, :] = jnp.exp(st[z, 0:4, :] - upper) / sum_total
    cs[4:8, :] = sum_inner / sum_total
    scale = jnp.concatenate([cs[t : t + 1, :] for t in range(4)], axis=1)
    ratio = jnp.concatenate([cs[t : t + 1, :] for t in range(4, 8)], axis=1)
    attention = es[...] * scale
    score_low = (attention * (dp[...] - ratio)).astype(BF16)
    attention_low = attention.astype(BF16)
    key_grad = jnp.dot(score_low, queries, preferred_element_type=F32) * factor
    value_grad = jnp.dot(attention_low, dout, preferred_element_type=F32)
    key_value = jnp.concatenate([key_grad, value_grad], axis=1).reshape(4, BLK, 256)
    dkvf[...] = key_value
    dkvp[...] = key_value.astype(BF16)

    def rs_copy(d):
        a, b = kv_peer(d)
        i = a * 2 + b
        return remote(dkvp.at[i], dkvr.at[own4], sem("rs_s"), sem("rs_r"), at(cid(a, z, b), h, v))

    each(1, 4, lambda d: rs_copy(d).start())

    ey_send(1)

    query_part = tn(score_low, keys)
    for t in range(NZ):
        dqp[t] = query_part[t * PIECE : t * PIECE + 64].astype(BF16)

    def dq_copy(j):
        zd = zpeer(j)
        return remote(dqp.at[zd], dqr.at[z], sem("dq_s"), sem("dq_r"), at(cid(xh, zd, k), h, v))

    far_first(lambda j: dq_copy(j).start())
    ey_send(2)
    ey_send(3)
    ey_send(4)
    ey_copy(1, 1).start()
    ey_copy(1, 2).start()
    arrived(three_halves, "w")
    each(1, NH, lambda j: w_pass(j).start())
    ey_relay(0)
    arrived(dkvr.at[pl.ds(0, 3)], "rs")
    mine = dkvf[own4]
    for d in range(1, 4):
        a, b = kv_peer(d)
        mine = mine + dkvr[a * 2 + b].astype(F32)
    mine = mine.astype(BF16)
    dkvg[b_me] = mine
    hg[h] = mine

    def gx_peer(d):
        return lax.rem(xh + lax.div(d, 2), 2), lax.rem(v + lax.rem(d, 2), 2)

    def gx_copy(d):
        a, e = gx_peer(d)
        return remote(
            dkvg.at[b_me], dkvg.at[b_me], sem("gx_s"), gx_r.at[xh * 2 + v],
            at(cid(a, z, k), h, e),
        )

    def gc_copy(d):
        a, e = gx_peer(d)
        i = bid(a, k, e)
        return remote(
            dkvg.at[i], dkvg.at[i], sem("gc_s"), sem("gc_r"), at(cid(xh, z, ko), h, v)
        )

    def h_copy(j):
        hd = lax.rem(h + j, NH)
        return remote(hg.at[h], hg.at[h], sem("h_s"), h_r.at[h], at(c, hd, v))

    each(1, 4, lambda d: gx_copy(d).start())
    each(1, NH, lambda j: h_copy(j).start())
    gc_copy(0).start()

    def forward(d):
        a, e = gx_peer(d)
        i = bid(a, k, e)
        remote(
            dkvg.at[i], dkvg.at[i], sem("gx_s"), gx_r.at[a * 2 + e], here
        ).wait_recv()
        gc_copy(d).start()

    ey_relay(1)
    ey_relay(2)
    ey_relay(3)
    ey_relay(4)

    def head_term(n):
        rows = pl.ds(pl.multiple_of(n * 896, 128), 896)
        return nt(hg[n], wb[rows, :]).astype(BF16).astype(F32)

    def h_arrived(j):
        n = lax.rem(h + j, NH)
        remote(hg.at[n], hg.at[n], sem("h_s"), h_r.at[n], here).wait_recv()

    loads[4].wait()
    terms_sum[...] = head_term(h)
    each(1, 4, forward)

    arrived(three_halves, "wf")
    h_arrived(1)
    h_arrived(3)
    summed = terms_sum[...] + head_term(up) + head_term(down)
    h_arrived(2)
    summed = summed + head_term(far)
    owners = jnp.full((BLK, 896), owner, jnp.int32)
    egs[0] = jnp.where(owners == c_next, summed, 0.0).astype(BF16)
    egs[1] = jnp.where(owners == c_next, 0.0, summed).astype(BF16)
    out_next = remote(
        egs.at[0], eg_ref.at[pl.ds(0, 128)], sem("o_s"), sem("o_r"), at(c_next, h, v)
    )
    out_prev = remote(
        egs.at[1], eg_ref.at[pl.ds(128, 128)], sem("o_s"), sem("o_r"), at(c_prev, h, v)
    )
    out_next.start()
    out_prev.start()

    arrived(dkvg.at[pl.ds(0, 4)], "gc")
    for i in range(5):
        ey_arrived(1 - pass_side(i), i)

    def quarter(n):
        turned = encb[n].reshape(128, 896).T
        rows = jnp.concatenate([turned[:448], turned[448:]], axis=1)
        grads = jnp.concatenate(
            [
                dkvg[i, pl.ds(pl.multiple_of(n * 32 + first, 16), 16), :]
                for first in (0, 16)
                for i in range(8)
            ],
            axis=0,
        )
        return jnp.dot(rows, grads, preferred_element_type=F32)

    acc = quarter(h) + quarter(up) + quarter(down)
    arrived(encb.at[far], "ep")
    acc = acc + quarter(far)
    for t in range(NZ):
        piece = acc[t * PIECE : (t + 1) * PIECE]
        wgs[t] = jnp.concatenate([piece[:, :128], piece[:, 128:]], axis=0).astype(BF16)

    def wg_copy(j):
        zd = zpeer(j)
        return remote(wgs.at[zd], wgr.at[z], sem("wg_s"), sem("wg_r"), at(cid(xh, zd, k), h, v))

    far_first(lambda j: wg_copy(j).start())

    arrived(dqr.at[pl.ds(0, 7)], "dq")
    query_grad = dqp[z].astype(F32)
    for j in range(1, NZ):
        query_grad = query_grad + dqr[zpeer(j)].astype(F32)
    query_grad = query_grad * factor
    dq_ref[...] = jnp.concatenate(
        [query_grad[g * 8 : (g + 1) * 8] for g in range(QPG)], axis=1
    ).astype(BF16)

    sent(qg.at[pl.ds(0, 7)], "q")
    sent(kb.at[pl.ds(0, 3)], "k")
    sent(vb.at[pl.ds(0, 3)], "v")
    sent(cand, "c")
    sent(three_halves, "w")
    sent(three_halves, "wf")
    sent(encb.at[h, pl.ds(0, 7)], "ex")
    sent(encb.at[h], "eu")
    sent(encb.at[h], "ed")
    sent(encb.at[h], "ep")
    sent(st.at[pl.ds(0, 7)], "st")
    sent(dkvp.at[pl.ds(0, 3)], "rs")
    sent(dqp.at[pl.ds(0, 7)], "dq")
    sent(dkvg.at[pl.ds(0, 3)], "gx")
    sent(dkvg.at[pl.ds(0, 4)], "gc")
    sent(hg.at[pl.ds(0, 3)], "h")

    arrived(wgr.at[pl.ds(0, 7)], "wg")
    weight = wgs[z].astype(F32)
    for j in range(1, NZ):
        weight = weight + wgr[zpeer(j)].astype(F32)
    wg_ref[...] = jnp.concatenate([weight[:PIECE], weight[PIECE:]], axis=1)

    arrived(egs, "o")
    sent(egs, "o")
    sent(wgs.at[pl.ds(0, 7)], "wg")


def copy_kernel(dq_in, eg_in, wg_in, dq_out, eg_out, wg_out, sems):
    pairs = ((dq_in, dq_out), (eg_in, eg_out), (wg_in, wg_out))
    moves = [pltpu.make_async_copy(a, b, sems.at[i]) for i, (a, b) in enumerate(pairs)]
    for move in moves:
        move.start()
    for move in moves:
        move.wait()


def finish(dq, eg, wg):
    hbm = pl.BlockSpec(memory_space=pl.ANY)
    arrays = tuple(pltpu.with_memory_space_constraint(a, pltpu.VMEM) for a in (dq, eg, wg))
    outs = pl.pallas_call(
        copy_kernel,
        out_shape=tuple(jax.ShapeDtypeStruct(a.shape, a.dtype) for a in arrays),
        in_specs=[pl.BlockSpec(memory_space=pltpu.VMEM)] * 3,
        out_specs=(hbm,) * 3,
        scratch_shapes=[pltpu.SemaphoreType.DMA((3,))],
    )(*arrays)
    return outs[0][None], outs[1][None], outs[2]


def per_device(queries, keys, values, dout, lengths, owner, enc_rows, w_kv):
    dma = pltpu.SemaphoreType.DMA
    vmem = pltpu.VMEM
    hbm = pl.BlockSpec(memory_space=pl.ANY)
    out = pl.BlockSpec(memory_space=pltpu.VMEM)
    dq, eg, wg = pl.pallas_call(
        kernel,
        out_shape=(
            vmem((8, 896), BF16),
            vmem((256, 896), BF16),
            vmem((PIECE, 256), F32),
        ),
        in_specs=[hbm] * 8,
        out_specs=(out, out, out),
        scratch_shapes=[
            pltpu.SMEM((1,), jnp.int32),
            pltpu.SMEM((1, 1), jnp.int32),
            vmem((8, 896), BF16),
            vmem((8, 896), BF16),
            vmem((NZ, 2 * PIECE, HD), BF16),
            vmem((4, BLK, HD), BF16),
            vmem((4, BLK, HD), BF16),
            vmem((2, 32, 3584), BF16),
            vmem((2, 4, 16, 896), BF16),
            vmem((NH, 8, 16, 896), BF16),
            vmem((NH * 896, 256), BF16),
            vmem((NZ, 12, 128), F32),
            vmem((8, 128), F32),
            vmem((512, 512), F32),
            vmem((512, 512), F32),
            vmem((4, BLK, 256), BF16),
            vmem((4, BLK, 256), BF16),
            vmem((4, BLK, 256), F32),
            vmem((8, BLK, 256), BF16),
            vmem((NH, BLK, 256), BF16),
            vmem((NZ, 64, HD), BF16),
            vmem((NZ, 64, HD), BF16),
            vmem((2, BLK, 896), BF16),
            vmem((NZ, 2 * PIECE, 128), BF16),
            vmem((NZ, 2 * PIECE, 128), BF16),
            vmem((BLK, 896), F32),
            dma((len(SEMS),)),
            dma((4,)),
            dma((4,)),
            dma((2, 5)),
            dma((4,)),
        ],
        compiler_params=pltpu.CompilerParams(
            collective_id=0, has_side_effects=True, vmem_limit_bytes=60 * 1024 * 1024
        ),
    )(queries[0], keys[0], values[0], dout[0], lengths, owner, enc_rows[0], w_kv)
    return finish(dq, eg, wg)


def solution(mesh):
    placed = (
        P("video", "ctx", "head"),
        P("video", "ctx", "head"),
        P("video", "ctx", "head"),
        P("video", "ctx", "head"),
        P("video"),
        P("video", "ctx"),
        P("video", "ctx", None),
        P(None, "head"),
    )
    return jax.shard_map(
        per_device,
        mesh=mesh,
        in_specs=placed,
        out_specs=(
            P("video", "ctx", "head"),
            P("video", "ctx", "head"),
            P(("ctx", "video"), "head"),
        ),
        check_vma=False,
    )
```

```python
import math

import jax
import jax.numpy as jnp
from jax import lax
from jax.experimental import pallas as pl
from jax.experimental.pallas import tpu as pltpu
from jax.sharding import PartitionSpec as P

NZ = 8
NC = 32
NH = 4
HD = 128
BLK = 128
QPG = 7
PIECE = 56
F32 = jnp.float32
BF16 = jnp.bfloat16
MESH = pl.DeviceIdType.MESH


SEMS = (
    "q", "k", "w", "small", "q_s", "q_r", "k_s", "k_r", "v_s", "v_r", "st_s", "st_r",
    "dq_s", "dq_r", "rs_s", "rs_r", "gx_s", "gc_s", "gc_r", "c_s", "c_r", "ex_s",
    "eu_s", "ed_s", "ep_s", "ep_r", "w_s", "w_r", "wf_s", "wf_r", "h_s",
    "o_s", "o_r", "wg_s", "wg_r", "do", "v", "own",
)


def each(start, stop, fn):
    def step(i, carry):
        fn(i)
        return carry

    lax.fori_loop(start, stop, step, 0)


def nt(a, b):
    return lax.dot_general(a, b, (((1,), (1,)), ((), ())), preferred_element_type=F32)


def tn(a, b):
    return lax.dot_general(a, b, (((0,), (0,)), ((), ())), preferred_element_type=F32)


def kernel(
    q_ref, k_ref, v_ref, do_ref, len_in, own_in, enc_ref, w_ref,
    dq_ref, eg_ref, wg_ref,
    len_ref, own_ref, qv, dov, qg, kb, vb, cand, encs, encb, wb, st, cs, es, dp,
    dkvp, dkvr, dkvf, dkvg, hg, dqp, dqr, egs, wgs, wgr,
    terms_sum, sems, gx_r, ex_r, ey_r, h_r,
):
    factor = 1.0 / math.sqrt(HD)
    c = lax.axis_index("ctx")
    h = lax.axis_index("head")
    v = lax.axis_index("video")
    xh, z, k = lax.div(c, 2 * NZ), lax.rem(lax.div(c, 2), NZ), lax.rem(c, 2)
    ko = 1 - k
    c_next, c_prev = lax.rem(c + 1, NC), lax.rem(c + NC - 1, NC)
    c_cross = lax.rem(c + 2 * k - 1 + NC, NC)

    def cid(a, b, d):
        return (a * NZ + b) * 2 + d

    def at(ctx, head, video):
        return {"ctx": ctx, "head": head, "video": video}

    def remote(src, dst, ssem, rsem, dev):
        return pltpu.make_async_remote_copy(
            src_ref=src, dst_ref=dst, send_sem=ssem, recv_sem=rsem,
            device_id=dev, device_id_type=MESH,
        )

    here = at(c, h, v)

    def sent(ref, name):
        remote(ref, ref, sem(name + "_s"), sem(name + "_s"), here).wait_send()

    def arrived(ref, name):
        remote(ref, ref, sem(name + "_r"), sem(name + "_r"), here).wait_recv()

    def sem(name):
        return sems.at[SEMS.index(name)]

    def zpeer(j):
        return lax.rem(z + j, NZ)

    def far_first(fn):
        def step(i):
            half = lax.div(i + 1, 2)
            fn(4 + half - 2 * half * lax.rem(i, 2))

        each(0, NZ - 1, step)

    def ppeer(d):
        return (
            lax.rem(xh + lax.div(d, 4), 2),
            lax.rem(k + lax.rem(lax.div(d, 2), 2), 2),
            lax.rem(v + lax.rem(d, 2), 2),
        )

    def bid(a, b, d):
        return a * 4 + d * 2 + b

    barrier = pltpu.get_barrier_semaphore()

    def signal(dev):
        pl.semaphore_signal(barrier, inc=1, device_id=dev, device_id_type=MESH)

    each(1, NZ, lambda j: signal(at(cid(xh, zpeer(j), k), h, v)))

    def sig_plane(d):
        a, b, e = ppeer(d)
        signal(at(cid(a, z, b), h, e))

    each(1, 8, sig_plane)

    signal(at(c_cross, h, v))
    each(1, NH, lambda j: signal(at(c, lax.rem(h + j, NH), v)))

    own4 = xh * 2 + k
    wrows = pl.ds(pl.multiple_of(h * 896, 128), 896)
    loads = [
        pltpu.make_async_copy(q_ref, qv, sem("q")),
        pltpu.make_async_copy(do_ref, dov, sem("do")),
        pltpu.make_async_copy(k_ref, kb.at[own4], sem("k")),
        pltpu.make_async_copy(v_ref, vb.at[own4], sem("v")),
        pltpu.make_async_copy(w_ref.at[wrows], wb.at[wrows], sem("w")),
        pltpu.make_async_copy(len_in, len_ref, sem("small")),
        pltpu.make_async_copy(own_in, own_ref, sem("own")),
    ]
    for load in loads:
        load.start()
    loads[0].wait()
    loads[1].wait()
    parts = []
    for ref in (qv, dov):
        rows = ref[...].astype(F32)
        parts += [rows[:, g * HD : (g + 1) * HD] for g in range(QPG)]
    qg[z] = jnp.concatenate(parts, axis=0).astype(BF16)

    pl.semaphore_wait(barrier, 18)

    def q_copy(j):
        zd = zpeer(j)
        return remote(qg.at[z], qg.at[z], sem("q_s"), sem("q_r"), at(cid(xh, zd, k), h, v))

    far_first(lambda j: q_copy(j).start())

    def cand_copy(side):
        slot, ctx = ((ko, cid(xh, z, ko)), (k, c_cross))[side]
        rows = pl.ds(pl.multiple_of(slot * BLK + h * 32, 32), 32)
        return remote(enc_ref.at[rows], cand.at[side], sem("c_s"), sem("c_r"), at(ctx, h, v))

    cand_copy(1).start()

    def kv_peer(d):
        return lax.rem(xh + lax.div(d, 2), 2), lax.rem(k + lax.rem(d, 2), 2)

    def kv_copy(d, side):
        a, b = kv_peer(d)
        src, dst = ((k_ref, kb), (v_ref, vb))[side]
        name = ("k", "v")[side]
        return remote(
            src, dst.at[own4], sem(name + "_s"), sem(name + "_r"), at(cid(a, z, b), h, v)
        )

    for side in (0, 1):
        each(1, 4, lambda d: kv_copy(d, side).start())

    cand_copy(0).start()

    def w_rows(hd, core):
        return pl.ds(pl.multiple_of(hd * 896 + core * 448, 64), 448)

    def w_copy(j):
        hd = lax.rem(h + j, NH)
        return remote(
            w_ref.at[w_rows(hd, k)], wb.at[w_rows(h, k)], sem("w_s"), sem("w_r"), at(c, hd, v)
        )

    def w_pass(j):
        part = wb.at[w_rows(lax.rem(h + j, NH), k)]
        return remote(part, part, sem("wf_s"), sem("wf_r"), at(cid(xh, z, ko), h, v))

    three_halves = wb.at[pl.ds(0, 3 * 448)]
    each(1, NH, lambda j: w_copy(j).start())

    loads[2].wait()
    loads[3].wait()
    loads[5].wait()
    loads[6].wait()
    arrived(kb.at[pl.ds(0, 3)], "k")
    arrived(vb.at[pl.ds(0, 3)], "v")
    arrived(qg.at[pl.ds(0, 7)], "q")
    keys = kb[...].reshape(512, HD)
    text = qg[...].astype(F32)
    rest = jnp.zeros((512 - NZ * PIECE, HD), F32)

    def text_rows(first):
        rows = text[:, first : first + PIECE].reshape(NZ * PIECE, HD)
        return jnp.concatenate([rows, rest], axis=0).astype(BF16)

    queries, dout = text_rows(0), text_rows(PIECE)
    block = lax.div(lax.broadcasted_iota(jnp.int32, (512, 512), 0), BLK)
    place = lax.div(block, 2) * (2 * NZ) + z * 2 + lax.rem(block, 2)
    valid = place < len_ref[0]
    masked = jnp.where(valid, nt(keys, queries) * factor, -1e30)
    top = jnp.max(masked, axis=0, keepdims=True)
    terms = jnp.where(valid, jnp.exp(masked - top), 0.0)
    grad_prob = nt(vb[...].reshape(512, HD), dout)
    es[...] = terms
    dp[...] = grad_prob
    total = jnp.sum(terms, axis=0, keepdims=True)
    inner = jnp.sum(terms * grad_prob, axis=0, keepdims=True)
    for n, value in enumerate((top, total, inner)):
        for t in range(4):
            st[z, n * 4 + t : n * 4 + t + 1, :] = value[:, t * 128 : (t + 1) * 128]

    def st_copy(j):
        zd = zpeer(j)
        return remote(st.at[z], st.at[z], sem("st_s"), sem("st_r"), at(cid(xh, zd, k), h, v))

    far_first(lambda j: st_copy(j).start())

    owner = own_ref[0, 0]
    b_me = bid(xh, k, v)
    arrived(cand, "c")
    same = jnp.full((32, 3584), owner, jnp.int32) == c + 1 - 2 * k
    chosen = jnp.where(same, cand[0].astype(F32), cand[1].astype(F32))
    for a in (0, 1):
        for t in range(4):
            starts = [a * 1792 + n * 4 * PIECE + t * PIECE for n in range(NZ)]
            pieces = [
                chosen[first : first + 16, start : start + PIECE]
                for first in (0, 16)
                for start in starts
            ]
            encs[a, t] = jnp.concatenate(pieces, axis=1).astype(BF16)

    def ex_copy(d):
        a, b, e = ppeer(d)
        return remote(
            encs.at[a, b * 2 + e], encb.at[h, b_me], sem("ex_s"), ex_r.at[xh * 2 + v],
            at(cid(a, z, b), h, e),
        )

    up, down, far = lax.rem(h + 1, NH), lax.rem(h + 3, NH), lax.rem(h + 2, NH)

    def chip(i):
        return lax.rem(xh + i // 2, 2), lax.rem(v + ((i + 1) // 2) % 2, 2)

    def chunk(hd, i):
        if i < 2:
            return encb.at[hd, pl.ds(bid(xh, (k, ko)[i], v), 1)]
        a, e = chip(i - 1)
        return encb.at[hd, pl.ds(bid(a, 0, e), 2)]

    def ey_copy(side, i):
        part = chunk(h, i)
        return remote(
            part, part, sem(("eu_s", "ed_s")[side]), ey_r.at[side, i], at(c, (up, down)[side], v)
        )

    def ey_arrived(side, i):
        part = chunk((down, up)[side], i)
        remote(part, part, sem("eu_s"), ey_r.at[side, i], here).wait_recv()

    def ey_send(i):
        if i > 0:
            a, e = chip(i - 1)
            part = chunk(h, i)
            remote(part, part, sem("ex_s"), ex_r.at[a * 2 + e], here).wait_recv()
        ey_copy(0, i).start()
        if i not in (1, 2):
            ey_copy(1, i).start()

    def pass_side(i):
        return 0 if i < 3 else 1

    def ey_pass(i):
        side = pass_side(i)
        part = chunk((down, up)[side], i)
        return remote(part, part, sem("ep_s"), sem("ep_r"), at(c, (up, down)[side], v))

    def ey_relay(i):
        ey_arrived(pass_side(i), i)
        ey_pass(i).start()

    encb[h, b_me] = encs[xh, k * 2 + v]
    ey_send(0)
    for d in (2, 1, 3, 5, 7, 4, 6):
        ex_copy(d).start()
    arrived(st.at[pl.ds(0, 7)], "st")
    tops, totals, inners = st[:, 0:4, :], st[:, 4:8, :], st[:, 8:12, :]
    upper = jnp.max(tops, axis=0)
    scales = jnp.exp(tops - upper[None])
    sum_total = jnp.sum(totals * scales, axis=0)
    sum_inner = jnp.sum(inners * scales, axis=0)
    cs[0:4, :] = jnp.exp(st[z, 0:4, :] - upper) / sum_total
    cs[4:8, :] = sum_inner / sum_total
    scale = jnp.concatenate([cs[t : t + 1, :] for t in range(4)], axis=1)
    ratio = jnp.concatenate([cs[t : t + 1, :] for t in range(4, 8)], axis=1)
    attention = es[...] * scale
    score_low = (attention * (dp[...] - ratio)).astype(BF16)
    attention_low = attention.astype(BF16)
    key_grad = jnp.dot(score_low, queries, preferred_element_type=F32) * factor
    value_grad = jnp.dot(attention_low, dout, preferred_element_type=F32)
    key_value = jnp.concatenate([key_grad, value_grad], axis=1).reshape(4, BLK, 256)
    dkvf[...] = key_value
    dkvp[...] = key_value.astype(BF16)

    def rs_copy(d):
        a, b = kv_peer(d)
        i = a * 2 + b
        return remote(dkvp.at[i], dkvr.at[own4], sem("rs_s"), sem("rs_r"), at(cid(a, z, b), h, v))

    each(1, 4, lambda d: rs_copy(d).start())

    ey_send(1)

    query_part = tn(score_low, keys)
    for t in range(NZ):
        dqp[t] = query_part[t * PIECE : t * PIECE + 64].astype(BF16)

    def dq_copy(j):
        zd = zpeer(j)
        return remote(dqp.at[zd], dqr.at[z], sem("dq_s"), sem("dq_r"), at(cid(xh, zd, k), h, v))

    far_first(lambda j: dq_copy(j).start())
    ey_send(2)
    ey_send(3)
    ey_send(4)
    ey_copy(1, 1).start()
    ey_copy(1, 2).start()
    arrived(three_halves, "w")
    each(1, NH, lambda j: w_pass(j).start())
    ey_relay(0)
    arrived(dkvr.at[pl.ds(0, 3)], "rs")
    mine = dkvf[own4]
    for d in range(1, 4):
        a, b = kv_peer(d)
        mine = mine + dkvr[a * 2 + b].astype(F32)
    mine = mine.astype(BF16)
    dkvg[b_me] = mine
    hg[h] = mine

    def gx_peer(d):
        return lax.rem(xh + lax.div(d, 2), 2), lax.rem(v + lax.rem(d, 2), 2)

    def gx_copy(d):
        a, e = gx_peer(d)
        return remote(
            dkvg.at[b_me], dkvg.at[b_me], sem("gx_s"), gx_r.at[xh * 2 + v],
            at(cid(a, z, k), h, e),
        )

    def gc_copy(d):
        a, e = gx_peer(d)
        i = bid(a, k, e)
        return remote(
            dkvg.at[i], dkvg.at[i], sem("gc_s"), sem("gc_r"), at(cid(xh, z, ko), h, v)
        )

    def h_copy(j):
        hd = lax.rem(h + j, NH)
        return remote(hg.at[h], hg.at[h], sem("h_s"), h_r.at[h], at(c, hd, v))

    each(1, 4, lambda d: gx_copy(d).start())
    each(1, NH, lambda j: h_copy(j).start())
    gc_copy(0).start()

    def forward(d):
        a, e = gx_peer(d)
        i = bid(a, k, e)
        remote(
            dkvg.at[i], dkvg.at[i], sem("gx_s"), gx_r.at[a * 2 + e], here
        ).wait_recv()
        gc_copy(d).start()

    ey_relay(1)
    ey_relay(2)
    ey_relay(3)
    ey_relay(4)

    def head_term(n):
        rows = pl.ds(pl.multiple_of(n * 896, 128), 896)
        return nt(hg[n], wb[rows, :]).astype(BF16).astype(F32)

    def h_arrived(j):
        n = lax.rem(h + j, NH)
        remote(hg.at[n], hg.at[n], sem("h_s"), h_r.at[n], here).wait_recv()

    loads[4].wait()
    terms_sum[...] = head_term(h)
    each(1, 4, forward)

    arrived(three_halves, "wf")
    h_arrived(1)
    h_arrived(3)
    summed = terms_sum[...] + head_term(up) + head_term(down)
    h_arrived(2)
    summed = summed + head_term(far)
    owners = jnp.full((BLK, 896), owner, jnp.int32)
    egs[0] = jnp.where(owners == c_next, summed, 0.0).astype(BF16)
    egs[1] = jnp.where(owners == c_next, 0.0, summed).astype(BF16)
    out_next = remote(
        egs.at[0], eg_ref.at[pl.ds(0, 128)], sem("o_s"), sem("o_r"), at(c_next, h, v)
    )
    out_prev = remote(
        egs.at[1], eg_ref.at[pl.ds(128, 128)], sem("o_s"), sem("o_r"), at(c_prev, h, v)
    )
    out_next.start()
    out_prev.start()

    arrived(dkvg.at[pl.ds(0, 4)], "gc")
    for i in range(5):
        ey_arrived(1 - pass_side(i), i)

    def quarter(n):
        turned = encb[n].reshape(128, 896).T
        rows = jnp.concatenate([turned[:448], turned[448:]], axis=1)
        grads = jnp.concatenate(
            [
                dkvg[i, pl.ds(pl.multiple_of(n * 32 + first, 16), 16), :]
                for first in (0, 16)
                for i in range(8)
            ],
            axis=0,
        )
        return jnp.dot(rows, grads, preferred_element_type=F32)

    acc = quarter(h) + quarter(up) + quarter(down)
    arrived(encb.at[far], "ep")
    acc = acc + quarter(far)
    for t in range(NZ):
        piece = acc[t * PIECE : (t + 1) * PIECE]
        wgs[t] = jnp.concatenate([piece[:, :128], piece[:, 128:]], axis=0).astype(BF16)

    def wg_copy(j):
        zd = zpeer(j)
        return remote(wgs.at[zd], wgr.at[z], sem("wg_s"), sem("wg_r"), at(cid(xh, zd, k), h, v))

    each(1, NZ, lambda j: wg_copy(j).start())

    arrived(dqr.at[pl.ds(0, 7)], "dq")
    query_grad = dqp[z].astype(F32)
    for j in range(1, NZ):
        query_grad = query_grad + dqr[zpeer(j)].astype(F32)
    query_grad = query_grad * factor
    dq_ref[...] = jnp.concatenate(
        [query_grad[g * 8 : (g + 1) * 8] for g in range(QPG)], axis=1
    ).astype(BF16)

    sent(qg.at[pl.ds(0, 7)], "q")
    sent(kb.at[pl.ds(0, 3)], "k")
    sent(vb.at[pl.ds(0, 3)], "v")
    sent(cand, "c")
    sent(three_halves, "w")
    sent(three_halves, "wf")
    sent(encb.at[h, pl.ds(0, 7)], "ex")
    sent(encb.at[h], "eu")
    sent(encb.at[h], "ed")
    sent(encb.at[h], "ep")
    sent(st.at[pl.ds(0, 7)], "st")
    sent(dkvp.at[pl.ds(0, 3)], "rs")
    sent(dqp.at[pl.ds(0, 7)], "dq")
    sent(dkvg.at[pl.ds(0, 3)], "gx")
    sent(dkvg.at[pl.ds(0, 4)], "gc")
    sent(hg.at[pl.ds(0, 3)], "h")

    arrived(wgr.at[pl.ds(0, 7)], "wg")
    weight = wgs[z].astype(F32)
    for j in range(1, NZ):
        weight = weight + wgr[zpeer(j)].astype(F32)
    wg_ref[...] = jnp.concatenate([weight[:PIECE], weight[PIECE:]], axis=1)

    arrived(egs, "o")
    sent(egs, "o")
    sent(wgs.at[pl.ds(0, 7)], "wg")


def copy_kernel(dq_in, eg_in, wg_in, dq_out, eg_out, wg_out, sems):
    pairs = ((dq_in, dq_out), (eg_in, eg_out), (wg_in, wg_out))
    moves = [pltpu.make_async_copy(a, b, sems.at[i]) for i, (a, b) in enumerate(pairs)]
    for move in moves:
        move.start()
    for move in moves:
        move.wait()


def finish(dq, eg, wg):
    hbm = pl.BlockSpec(memory_space=pl.ANY)
    arrays = tuple(pltpu.with_memory_space_constraint(a, pltpu.VMEM) for a in (dq, eg, wg))
    outs = pl.pallas_call(
        copy_kernel,
        out_shape=tuple(jax.ShapeDtypeStruct(a.shape, a.dtype) for a in arrays),
        in_specs=[pl.BlockSpec(memory_space=pltpu.VMEM)] * 3,
        out_specs=(hbm,) * 3,
        scratch_shapes=[pltpu.SemaphoreType.DMA((3,))],
    )(*arrays)
    return outs[0][None], outs[1][None], outs[2]


def per_device(queries, keys, values, dout, lengths, owner, enc_rows, w_kv):
    dma = pltpu.SemaphoreType.DMA
    vmem = pltpu.VMEM
    hbm = pl.BlockSpec(memory_space=pl.ANY)
    out = pl.BlockSpec(memory_space=pltpu.VMEM)
    dq, eg, wg = pl.pallas_call(
        kernel,
        out_shape=(
            vmem((8, 896), BF16),
            vmem((256, 896), BF16),
            vmem((PIECE, 256), F32),
        ),
        in_specs=[hbm] * 8,
        out_specs=(out, out, out),
        scratch_shapes=[
            pltpu.SMEM((1,), jnp.int32),
            pltpu.SMEM((1, 1), jnp.int32),
            vmem((8, 896), BF16),
            vmem((8, 896), BF16),
            vmem((NZ, 2 * PIECE, HD), BF16),
            vmem((4, BLK, HD), BF16),
            vmem((4, BLK, HD), BF16),
            vmem((2, 32, 3584), BF16),
            vmem((2, 4, 16, 896), BF16),
            vmem((NH, 8, 16, 896), BF16),
            vmem((NH * 896, 256), BF16),
            vmem((NZ, 12, 128), F32),
            vmem((8, 128), F32),
            vmem((512, 512), F32),
            vmem((512, 512), F32),
            vmem((4, BLK, 256), BF16),
            vmem((4, BLK, 256), BF16),
            vmem((4, BLK, 256), F32),
            vmem((8, BLK, 256), BF16),
            vmem((NH, BLK, 256), BF16),
            vmem((NZ, 64, HD), BF16),
            vmem((NZ, 64, HD), BF16),
            vmem((2, BLK, 896), BF16),
            vmem((NZ, 2 * PIECE, 128), BF16),
            vmem((NZ, 2 * PIECE, 128), BF16),
            vmem((BLK, 896), F32),
            dma((len(SEMS),)),
            dma((4,)),
            dma((4,)),
            dma((2, 5)),
            dma((4,)),
        ],
        compiler_params=pltpu.CompilerParams(
            collective_id=0, has_side_effects=True, vmem_limit_bytes=60 * 1024 * 1024
        ),
    )(queries[0], keys[0], values[0], dout[0], lengths, owner, enc_rows[0], w_kv)
    return finish(dq, eg, wg)


def solution(mesh):
    placed = (
        P("video", "ctx", "head"),
        P("video", "ctx", "head"),
        P("video", "ctx", "head"),
        P("video", "ctx", "head"),
        P("video"),
        P("video", "ctx"),
        P("video", "ctx", None),
        P(None, "head"),
    )
    return jax.shard_map(
        per_device,
        mesh=mesh,
        in_specs=placed,
        out_specs=(
            P("video", "ctx", "head"),
            P("video", "ctx", "head"),
            P(("ctx", "video"), "head"),
        ),
        check_vma=False,
    )
```
